512 devices in a mesh: orbit: 8 (over z), lon: 16 (over y, core), lat: 4 (over x).
Axes of the slice: x: 4, y: 8, z: 8, core: 2. Of those that a mesh axis runs over, the one named last changes fastest.
Arguments:
- observed: float32 [65536, 64], P(('orbit', 'lon', 'lat')), may hold values from -6 to 6
- ray_start: int32 [65536], P(('orbit', 'lon', 'lat')), may hold values from 0 to 2
- tile_cells: int32 [327680, 16], P(('orbit', 'lon', 'lat')), may hold values from 0 to 4095, as said below
- tile_lengths: float32 [327680, 16], P(('orbit', 'lon', 'lat')), may hold values from 0.05 to 0.2
- channel_kernel: float32 [7, 64], replicated, may hold values from -0.75 to 0.75
- noise_weight: float32 [64], replicated, may hold values from 0.25 to 4
- prior_weight: float32 [7], replicated, may hold values from 0.05 to 0.5
Outputs:
- solution_field: float32 [7, 64, 32, 128], P(None, 'lon', 'lat')
- residual: float32 [7, 64, 32, 128], P(None, 'lon', 'lat')
The draws below stay inside these ranges and needn't reach their ends.
Inputs may be any that keep to these rules, and one draw needn't show every extreme that they name: `tile_cells`: each row is a path through the block: its segments move across the block's longitudes at one latitude, their level falling to a tangent level and rising again, one level a segment.
All inputs are finite; a program needn't handle non-finite values.
Results may differ from the reference program's by a relative error of at most 0.0045.
Values sent between devices are 32-bit elements; how exact they have to be, the bound alone decides.
No kernel may reach another device: no remote copies, remote signals or barrier semaphores. Data moves between devices by JAX's collectives and lax.ppermute only.
A program may use at most 64 MiB of HBM per device.

```python
import math
import jax
import jax.numpy as jnp
from jax import lax

S = 7
CH = 64
CLON = 4
CLAT = 8
LEV = 128
RAY_DEV = 128
NT = 3
TILE = 16
ITERS = 4
SPAN = 5
NLON = 64
NLAT = 32
NRAY = 65536
N_ORBIT = 8
N_LON = 16
N_LAT = 4


def draw_tile_cells(key, part):
    row_count = N_ORBIT * N_LON * N_LAT * (2 * NT - 1) * RAY_DEV
    keys = jax.random.split(key, 4)
    lat_pick = jax.random.randint(keys[0], (row_count, 1), 0, CLAT)
    lowest = jax.random.randint(keys[1], (row_count, 1), 0, LEV - TILE + 1)
    turning = jax.random.randint(keys[2], (row_count, 1), 0, TILE)
    flipped = jax.random.randint(keys[3], (row_count, 1), 0, 2)
    steps = jnp.arange(TILE, dtype=jnp.int32)[None, :]
    column = steps * CLON // TILE
    column = jnp.where(flipped == 1, CLON - 1 - column, column)
    level = lowest + jnp.abs(steps - turning)
    return ((column * CLAT + lat_pick) * LEV + level).astype(jnp.int32)


def set_ends(entries, own_key, low, largest):
    extent = entries.shape
    spot = [jax.random.randint(jax.random.fold_in(own_key, axis), (), 0, extent[axis]) for axis in range(len(extent))]
    entries = entries.at[tuple(spot)].set(low)
    longest = extent.index(max(extent))
    spot[longest] = (spot[longest] + 1) % extent[longest]
    return entries.at[tuple(spot)].set(largest)


def steps_of(stream_key, extent, pieces, least, largest):
    loudness = 1.0
    for axis_at, blocks in pieces:
        steps = jax.random.uniform(jax.random.fold_in(jax.random.fold_in(stream_key, 6), axis_at), (blocks,), jnp.float32, least / len(pieces), largest / len(pieces))
        loudness = loudness * jnp.repeat(jnp.exp(steps), extent[axis_at] // blocks).reshape((-1,) + (1,) * (len(extent) - 1 - axis_at))
    return loudness


def scatter_about(rng, shape, deviation, limit, shards=(), kind=jnp.bfloat16):
    loudness = steps_of(rng, shape, shards, -0.22, 0.18) if shards else 1.0
    entries = jax.random.normal(rng, shape, jnp.float32) * deviation * loudness
    return jnp.minimum(jnp.maximum(entries, -limit), limit).astype(kind)


def setup_inputs(seed: int = 0) -> dict:
    key_of = jax.random.split(jax.random.key(seed), 8)
    observed = scatter_about(key_of[0], (NRAY, CH), 1.0, 6.0, ((0, 512),), jnp.float32)
    ray_start = set_ends(jax.random.randint(key_of[1], (NRAY,), 0, NT), jax.random.fold_in(key_of[1], 1), 0, NT - 1).astype(jnp.int32)
    tile_cells = draw_tile_cells(jax.random.fold_in(key_of[7], 71), 0)
    tile_lengths = jnp.clip(0.05 + 0.15 * jax.random.uniform(key_of[3], (NRAY * SPAN, TILE), jnp.float32) ** steps_of(key_of[3], (NRAY * SPAN, TILE), ((0, 512),), -0.2, 0.2), 0.05, 0.2)
    channel_kernel = scatter_about(key_of[4], (S, CH), CH ** -0.5, 0.75, (), jnp.float32)
    noise_weight = jnp.clip(jnp.exp(jax.random.uniform(key_of[5], (CH,), jnp.float32, math.log(0.25), math.log(4.0))), 0.25, 4.0)
    prior_weight = jnp.clip(jnp.exp(jax.random.uniform(key_of[6], (S,), jnp.float32, math.log(0.05), math.log(0.5))), 0.05, 0.5)
    return dict(observed=observed, ray_start=ray_start, tile_cells=tile_cells, tile_lengths=tile_lengths, channel_kernel=channel_kernel, noise_weight=noise_weight, prior_weight=prior_weight)


highest = lax.Precision.HIGHEST


def reference(observed, ray_start, tile_cells, tile_lengths, channel_kernel, noise_weight, prior_weight):
    reach = NT - 1
    span = 2 * NT - 1
    cell_count = CLON * CLAT * LEV
    weighted = channel_kernel * noise_weight[None, :]
    channel_gram = jnp.dot(weighted, channel_kernel.T, precision=highest)
    cell_table = tile_cells.reshape(N_ORBIT, N_LON, N_LAT, span, RAY_DEV, TILE)
    length_table = tile_lengths.reshape(N_ORBIT, N_LON, N_LAT, span, RAY_DEV, TILE)
    starts = ray_start.reshape(N_ORBIT, N_LON, N_LAT, RAY_DEV)
    lon_ids = jnp.arange(N_LON, dtype=jnp.int32)[:, None]
    lat_ids = jnp.arange(N_LAT, dtype=jnp.int32)[None, :]
    block_base = ((lon_ids * N_LAT + lat_ids) * cell_count).astype(jnp.int32)
    places = [(block_base[None, :, :, None, None] + cell_table[:, :, :, slot]).astype(jnp.int32) for slot in range(span)]
    lengths = [length_table[:, :, :, slot] for slot in range(span)]
    present = [((starts <= slot) & (starts + reach >= slot)).astype(jnp.float32) for slot in range(span)]
    ray_shape = (S, N_ORBIT, N_LON, N_LAT, RAY_DEV)

    def project(flat_field):
        total = jnp.zeros(ray_shape, jnp.float32)
        for slot in range(span):
            sums = jnp.sum(flat_field[:, places[slot]] * lengths[slot][None], axis=-1)
            sums = jnp.roll(sums, -(slot - reach), axis=2)
            total = total + sums * present[slot][None]
        return total

    def back(ray_image):
        summed = jnp.zeros((S, N_LON * N_LAT * cell_count), jnp.float32)
        for slot in range(span):
            moved = jnp.roll(ray_image * present[slot][None], slot - reach, axis=2)
            amounts = moved[..., None] * lengths[slot][None]
            summed = summed.at[:, places[slot].reshape(-1)].add(amounts.reshape(S, -1))
        return summed

    def to_grid(flat_field):
        shaped = flat_field.reshape(S, N_LON, N_LAT, CLON, CLAT, LEV).transpose(0, 1, 3, 2, 4, 5)
        return shaped.reshape(S, NLON, NLAT, LEV)

    def to_flat(field_value):
        shaped = field_value.reshape(S, N_LON, CLON, N_LAT, CLAT, LEV).transpose(0, 1, 3, 2, 4, 5)
        return shaped.reshape(S, N_LON * N_LAT * cell_count)

    def prior(field_value):
        padded = jnp.pad(field_value, ((0, 0), (0, 0), (1, 1), (1, 1)))
        neighbours = jnp.roll(field_value, 1, axis=1) + jnp.roll(field_value, -1, axis=1)
        neighbours = neighbours + padded[:, :, 2:, 1:-1] + padded[:, :, :-2, 1:-1]
        neighbours = neighbours + padded[:, :, 1:-1, 2:] + padded[:, :, 1:-1, :-2]
        return prior_weight[:, None, None, None] * (6.0 * field_value - neighbours)

    def operate(field_value):
        projected = project(to_flat(field_value))
        ray_image = jnp.dot(channel_gram, projected.reshape(S, -1), precision=highest).reshape(ray_shape)
        return to_grid(back(ray_image)) + prior(field_value)

    ray_source = lax.dot_general(weighted, observed, (((1,), (1,)), ((), ())), precision=highest)
    right_side = to_grid(back(ray_source.reshape(ray_shape)))
    solution_field = jnp.zeros_like(right_side)
    residual = right_side
    direction = right_side
    norm_now = jnp.sum(residual * residual)
    for turn_index in range(ITERS):
        image_field = operate(direction)
        step_size = norm_now / jnp.sum(direction * image_field)
        solution_field = solution_field + step_size * direction
        residual = residual - step_size * image_field
        norm_next = jnp.sum(residual * residual)
        direction = residual + (norm_next / norm_now) * direction
        norm_now = norm_next
    return solution_field, residual
```

```python
import jax
import jax.numpy as jnp
from jax import lax
from jax.experimental import pallas as pl
from jax.experimental.pallas import tpu as pltpu
from jax.sharding import PartitionSpec as P

S = 7
CLON = 4
CLAT = 8
LEV = 128
NT = 3
TILE = 16
ITERS = 4
SPAN = 5
ORB = 8
RAYS = 128
SLOT = ORB * RAYS
CELL = CLON * LEV
SHARD = SPAN * 2 * TILE + 8
F32 = jnp.float32
BF16 = jnp.bfloat16
highest = lax.Precision.HIGHEST
VMEM = pltpu.VMEM
LIMIT = pltpu.CompilerParams(vmem_limit_bytes=48 << 20)


def vspec():
    return pl.BlockSpec(memory_space=pltpu.VMEM)


def sspec():
    return pl.BlockSpec(memory_space=pltpu.SMEM)


def shift(block, axis, distance):
    size = lax.axis_size(axis)
    return lax.ppermute(block, axis, [(i, (i + distance) % size) for i in range(size)])


def split(values):
    high = values.astype(BF16)
    low = (values - high.astype(F32)).astype(BF16)
    return high, low


def start_kernel(prior_ref, obs_ref, start_ref, cells_ref, lengths_ref, kern_ref, noise_ref, shard_ref, gram_ref, prior_out, scale_out, pad):
    for slot in range(SPAN):
        rows = pl.ds(slot * RAYS, RAYS)
        base = slot * 2 * TILE
        shard_ref[base:base + TILE, :] = cells_ref[rows, :].astype(F32).T
        shard_ref[base + TILE:base + 2 * TILE, :] = lengths_ref[rows, :].T
    pad[...] = jnp.zeros_like(pad)
    pad[0:S, :] = kern_ref[...]
    kern = pad[...]
    weighted = kern * noise_ref[...]
    source = lax.dot_general(weighted, obs_ref[...], (((1,), (1,)), ((), ())), precision=highest, preferred_element_type=F32)
    base = SPAN * 2 * TILE
    sub = lax.broadcasted_iota(jnp.int32, (8, RAYS), 0)
    start = jnp.broadcast_to(start_ref[...].astype(F32), (8, RAYS))
    shard_ref[base:base + 8, :] = jnp.where(sub == S, start, source)
    wide = jnp.concatenate([kern] * CLAT, axis=0)
    wide_weighted = jnp.concatenate([weighted] * CLAT, axis=0)
    gram = lax.dot_general(wide_weighted, wide, (((1,), (1,)), ((), ())), precision=highest, preferred_element_type=F32)
    row = lax.broadcasted_iota(jnp.int32, gram.shape, 0)
    col = lax.broadcasted_iota(jnp.int32, gram.shape, 1)
    trace = jnp.sum(jnp.where((row == col) & (row < 8), gram, 0.0))
    top = prior_ref[0]
    for s in range(1, S):
        top = jnp.maximum(top, prior_ref[s])
    bound = jnp.full((8, 128), trace * 128.0 + 12.0 * top, F32)
    scale = 1.0 / bound
    scale_out[...] = scale
    gram_ref[...] = jnp.where((row >> 3) == (col >> 3), gram, 0.0) * scale[0:1, 0:1]
    species = lax.broadcasted_iota(jnp.int32, (CLAT * 8, 128), 0) & 7
    prior = jnp.zeros((CLAT * 8, 128), F32)
    for s in range(S):
        prior = jnp.where(species == s, prior_ref[s], prior)
    prior_out[...] = prior * scale[0:1, 0:1]


def gather_kernel(orbit_ref, *refs):
    shards, out = refs[:ORB], refs[ORB]
    base = SPAN * 2 * TILE
    for k in range(ORB):
        spot = lax.rem(orbit_ref[0] + (ORB - k), ORB)
        out[:, pl.ds(pl.multiple_of(spot * RAYS, RAYS), RAYS)] = shards[k][base:base + 8, :]


def build_kernel(orbit_ref, *refs):
    shards, (w_ref, lat_ref) = refs[:ORB], refs[ORB:]
    sub = lax.broadcasted_iota(jnp.int32, (8, RAYS), 0)
    odd = (sub & 1) == 1
    for k in range(ORB):
        spot = pl.multiple_of(lax.rem(orbit_ref[0] + (ORB - k), ORB) * RAYS, RAYS)

        def slot_body(slot, carry):
            base = pl.multiple_of(slot * 2 * TILE, 2 * TILE)
            cells = shards[k][pl.ds(base, TILE), :].astype(jnp.int32)
            lengths = shards[k][pl.ds(base + TILE, TILE), :]
            lat_ref[slot, :, pl.ds(spot, RAYS)] = jnp.broadcast_to((cells[0:1, :] >> 7) & 7, (8, RAYS))
            places = ((cells >> 10) << 7) | (cells & 127)
            first = jnp.broadcast_to(cells[0:1, :] & 1, (8, RAYS)) == 1
            swap = first != odd
            keys = []
            sizes = []
            for j in range(TILE // 2):
                even_key = jnp.broadcast_to(places[2 * j:2 * j + 1, :], (8, RAYS))
                odd_key = jnp.broadcast_to(places[2 * j + 1:2 * j + 2, :], (8, RAYS))
                keys.append(jnp.where(swap, odd_key, even_key) - sub)
                even_len = jnp.broadcast_to(lengths[2 * j:2 * j + 1, :], (8, RAYS))
                odd_len = jnp.broadcast_to(lengths[2 * j + 1:2 * j + 2, :], (8, RAYS))
                sizes.append(jnp.where(swap, odd_len, even_len))
            for pair in range(CELL // 16):
                parts = []
                for half in range(2):
                    offset = pair * 16 + half * 8
                    terms = [jnp.where(key == offset, size, 0.0) for key, size in zip(keys, sizes)]
                    while len(terms) > 1:
                        terms = [a + b for a, b in zip(terms[::2], terms[1::2])]
                    parts.append(terms[0])
                high, low = split(jnp.concatenate(parts, axis=0))
                w_ref[slot, pl.ds(pair * 16, 16), pl.ds(spot, RAYS)] = high
                w_ref[slot, pl.ds(CELL + pair * 16, 16), pl.ds(spot, RAYS)] = low
            return carry

        lax.fori_loop(0, SPAN, slot_body, 0)


def masked_rows(values, lat):
    rows = jnp.concatenate([jnp.where(lat == l, values, 0.0) for l in range(CLAT)], axis=0)
    return jnp.concatenate(split(rows), axis=0)


def back_all(sums, lats, w_ref):
    total = None
    for slot in range(SPAN):
        part = lax.dot_general(
            masked_rows(sums[slot], lats[slot]), w_ref[slot], (((1,), (1,)), ((), ())), preferred_element_type=F32
        )
        total = part if total is None else total + part
    total = total[:, :CELL] + total[:, CELL:]
    return total[:64] + total[64:]


def project_all(v, lats, w_ref, outs):
    own_ref, left_ref, right_ref, left2_ref, right2_ref, down_ref, up_ref = outs
    halves = jnp.concatenate(split(v), axis=0)
    rows = jnp.concatenate([halves, halves], axis=1)
    for slot in range(SPAN):
        wide = jnp.dot(rows, w_ref[slot], preferred_element_type=F32)
        wide = wide[:64] + wide[64:]
        lat = lats[slot]
        total = jnp.where(lat == 0, wide[0:8], 0.0)
        for l in range(1, CLAT):
            total = total + jnp.where(lat == l, wide[8 * l:8 * l + 8], 0.0)
        own_ref[slot] = total
        if slot >= 1:
            left_ref[slot - 1] = total
        if slot <= 3:
            right_ref[slot] = total
        if slot >= 2:
            left2_ref[slot - 2] = total
        if slot <= 2:
            right2_ref[slot] = total
    for l in range(CLAT):
        left_ref[4, :, pl.ds(l * LEV, LEV)] = v[8 * l:8 * l + 8, 0:LEV]
        right_ref[4, :, pl.ds(l * LEV, LEV)] = v[8 * l:8 * l + 8, CELL - LEV:]
    down_ref[...] = v[0:8]
    up_ref[...] = v[56:64]


def init_kernel(z2, z0, z1, z3, z4, lat_ref, w_ref, v_ref, mask_ref, *outs):
    sums, lats = [], []
    for slot, z in enumerate((z0, z1, z2, z3, z4)):
        begin = jnp.broadcast_to(z[S:S + 1, :], (8, SLOT))
        present = (begin <= slot) & (begin + (NT - 1) >= slot)
        lat = jnp.where(present, lat_ref[slot], -1)
        mask_ref[slot] = lat
        lats.append(lat)
        sub = lax.broadcasted_iota(jnp.int32, (8, SLOT), 0)
        sums.append(jnp.where(sub < S, z[...], 0.0))
    v = back_all(sums, lats, w_ref)
    v_ref[...] = v
    project_all(v, lats, w_ref, outs)


def next_vector(v_ref, own_ref, plus1, minus1, plus2, minus2, south, north, mask_ref, w_ref, gram_ref, prior_ref):
    sums = []
    for slot in range(SPAN):
        total = own_ref[slot]
        if slot <= 3:
            total = total + plus1[slot]
        if slot >= 1:
            total = total + minus1[slot - 1]
        if slot <= 2:
            total = total + plus2[slot]
        if slot >= 2:
            total = total + minus2[slot - 2]
        sums.append(total)
    lats = [mask_ref[slot] for slot in range(SPAN)]
    image = back_all(sums, lats, w_ref)
    image = jnp.dot(gram_ref[...], image, precision=highest, preferred_element_type=F32)
    v = v_ref[...]
    west = jnp.concatenate([minus1[4, :, l * LEV:(l + 1) * LEV] for l in range(CLAT)], axis=0)
    east = jnp.concatenate([plus1[4, :, l * LEV:(l + 1) * LEV] for l in range(CLAT)], axis=0)
    cols = [west] + [v[:, c * LEV:(c + 1) * LEV] for c in range(CLON)] + [east]
    lane = lax.broadcasted_iota(jnp.int32, (64, LEV), 1)
    pieces = []
    for c in range(CLON):
        here = cols[c + 1]
        below = jnp.where(lane == 0, 0.0, pltpu.roll(here, 1, 1))
        above = jnp.where(lane == LEV - 1, 0.0, pltpu.roll(here, LEV - 1, 1))
        south_side = jnp.concatenate([south[:, c * LEV:(c + 1) * LEV], here[:56]], axis=0)
        north_side = jnp.concatenate([here[8:], north[:, c * LEV:(c + 1) * LEV]], axis=0)
        near = cols[c] + cols[c + 2] + below + above + south_side + north_side
        pieces.append(prior_ref[...] * (6.0 * here - near))
    return image + jnp.concatenate(pieces, axis=1), lats


def step_kernel(*refs):
    v, lats = next_vector(*refs[:12])
    refs[12][...] = v
    project_all(v, lats, refs[9], refs[13:])


PAIRS = [(i, j) for i in range(ITERS + 1) for j in range(i, ITERS + 1) if (i, j) != (ITERS, ITERS)]


def last_kernel(*refs):
    v, _ = next_vector(*refs[:12])
    earlier = refs[12:12 + ITERS - 1]
    out_ref, pair_ref = refs[12 + ITERS - 1:]
    out_ref[...] = v
    vectors = [ref[...] for ref in earlier] + [refs[0][...], v]
    pair_ref[...] = jnp.zeros_like(pair_ref)
    for n, (i, j) in enumerate(PAIRS):
        product = vectors[i] * vectors[j]
        product = jnp.sum(product, axis=0, keepdims=True)
        fold = product[:, 0:LEV]
        for c in range(1, CLON):
            fold = fold + product[:, c * LEV:(c + 1) * LEV]
        pair_ref[n:n + 1, :] = fold


def combine_kernel(scale_ref, *refs):
    sums_ref, vector_refs, (x_ref, r_ref, spread) = refs[0], refs[1:ITERS + 2], refs[ITERS + 2:]
    sums = jnp.sum(sums_ref[...], axis=1, keepdims=True)
    table = {}
    for n, (i, j) in enumerate(PAIRS):
        table[i, j] = table[j, i] = sums[n:n + 1, :]
    scale = scale_ref[0:1, 0:1]
    zero, one = jnp.zeros((1, 1), F32), jnp.ones((1, 1), F32)
    x = [zero] * (ITERS + 1)
    r = [one] + [zero] * ITERS
    d = list(r)

    def form(a, b, na, nb, off):
        total = None
        for i in range(na):
            inner = None
            for j in range(nb):
                term = b[j] * table[i, j + off]
                inner = term if inner is None else inner + term
            term = a[i] * inner
            total = term if total is None else total + term
        return total

    norm = table[0, 0]
    for k in range(ITERS):
        alpha = norm / form(d, d, k + 1, k + 1, 1)
        for i in range(k + 1):
            x[i] = x[i] + alpha * d[i]
            r[i + 1] = r[i + 1] - alpha * d[i]
        if k < ITERS - 1:
            after = form(r, r, k + 2, k + 2, 0)
            ratio = after / norm
            d = [r[i] + ratio * d[i] for i in range(ITERS + 1)]
            norm = after
    x = [scale * value for value in x]
    for c in range(CLON):
        parts = [ref[:, c * LEV:(c + 1) * LEV] for ref in vector_refs]
        total = x[0] * parts[0]
        for i in range(1, ITERS):
            total = total + x[i] * parts[i]
        spread[0, c] = total
        total = r[0] * parts[0]
        for i in range(1, ITERS + 1):
            total = total + r[i] * parts[i]
        spread[1, c] = total
        for s in range(S):
            x_ref[s, c] = spread[0, c, pl.ds(s, CLAT, stride=8), :]
            r_ref[s, c] = spread[1, c, pl.ds(s, CLAT, stride=8), :]


def shape(*dims, dtype=F32):
    return jax.ShapeDtypeStruct(dims, dtype)


def call(kernel, outs, n_in, scalar=False, scratch=()):
    return pl.pallas_call(
        kernel,
        out_shape=outs,
        in_specs=([sspec()] if scalar else []) + [vspec()] * n_in,
        out_specs=[vspec()] * len(outs),
        scratch_shapes=scratch,
        compiler_params=LIMIT,
    )


SENT = (
    shape(SPAN, 8, SLOT), shape(5, 8, SLOT), shape(5, 8, SLOT), shape(3, 8, SLOT), shape(3, 8, SLOT), shape(8, CELL), shape(8, CELL),
)


def exchange(own, left, right, left2, right2, down, up):
    n_lat = lax.axis_size("lat")
    plus2 = shift(left2, "lon", -2)
    minus2 = shift(right2, "lon", 2)
    plus1 = shift(left, "lon", -1)
    minus1 = shift(right, "lon", 1)
    south = lax.ppermute(up, "lat", [(i, i + 1) for i in range(n_lat - 1)])
    north = lax.ppermute(down, "lat", [(i + 1, i) for i in range(n_lat - 1)])
    return own, plus1, minus1, plus2, minus2, south, north


def total_over(array, axis):
    size = lax.axis_size(axis)
    step = 1
    while step < size:
        others = [shift(array, axis, step * k) for k in (1, 2, 3)]
        array = (array + others[0]) + (others[1] + others[2])
        step *= 4
    return array


def body(observed, ray_start, tile_cells, tile_lengths, channel_kernel, noise_weight, prior_weight):
    orbit = lax.axis_index("orbit").astype(jnp.int32).reshape(1)
    shard, gram, prior, scale = call(
        start_kernel,
        (shape(SHARD, RAYS), shape(64, 64), shape(64, LEV), shape(8, LEV)),
        6,
        True,
        [pltpu.VMEM((8, 64), F32)],
    )(prior_weight, observed, ray_start.reshape(1, RAYS), tile_cells, tile_lengths, channel_kernel, noise_weight.reshape(1, -1))
    shards = [shard] + [shift(shard, "orbit", k) for k in range(1, ORB)]
    (z,) = call(gather_kernel, (shape(8, SLOT),), ORB, True)(orbit, *shards)
    z1, z3 = shift(z, "lon", -1), shift(z, "lon", 1)
    z0, z4 = shift(z, "lon", -2), shift(z, "lon", 2)
    w, lat = call(
        build_kernel, (shape(SPAN, 2 * CELL, SLOT, dtype=BF16), shape(SPAN, 8, SLOT, dtype=jnp.int32)), ORB, True
    )(orbit, *shards)
    v, mask, *sent = call(init_kernel, (shape(64, CELL), shape(SPAN, 8, SLOT, dtype=jnp.int32)) + SENT, 7)(z, z0, z1, z3, z4, lat, w)
    vectors = [v]
    for turn in range(ITERS - 1):
        v, *sent = call(step_kernel, (shape(64, CELL),) + SENT, 12)(v, *exchange(*sent), mask, w, gram, prior)
        vectors.append(v)
    v, pairs = call(last_kernel, (shape(64, CELL), shape(16, LEV)), 12 + ITERS - 1)(
        v, *exchange(*sent), mask, w, gram, prior, *vectors[:-1]
    )
    vectors.append(v)
    pairs = total_over(total_over(pairs, "lat"), "lon")
    field = shape(S, CLON, CLAT, LEV)
    return tuple(call(combine_kernel, (field, field), ITERS + 3, False, [pltpu.VMEM((2, CLON, 64, LEV), F32)])(scale, pairs, *vectors))


def solution(mesh):
    return jax.shard_map(
        body,
        mesh=mesh,
        in_specs=(
            P(("orbit", "lon", "lat"), None),
            P(("orbit", "lon", "lat")),
            P(("orbit", "lon", "lat"), None),
            P(("orbit", "lon", "lat"), None),
            P(),
            P(),
            P(),
        ),
        out_specs=(P(None, "lon", "lat", None), P(None, "lon", "lat", None)),
        check_vma=False,
    )
```

```python
import jax
import jax.numpy as jnp
from jax import lax
from jax.experimental import pallas as pl
from jax.experimental.pallas import tpu as pltpu
from jax.sharding import PartitionSpec as P

S = 7
CLON = 4
CLAT = 8
LEV = 128
NT = 3
TILE = 16
ITERS = 4
SPAN = 5
ORB = 8
RAYS = 128
SLOT = ORB * RAYS
CELL = CLON * LEV
CHAN = 64
SHARD = SPAN * 2 * TILE + 8
F32 = jnp.float32
BF16 = jnp.bfloat16
highest = lax.Precision.HIGHEST
VMEM = pltpu.VMEM
LIMIT = pltpu.CompilerParams(vmem_limit_bytes=24 << 20)


def vspec():
    return pl.BlockSpec(memory_space=pltpu.VMEM)


def sspec():
    return pl.BlockSpec(memory_space=pltpu.SMEM)


def shift(block, axis, distance):
    size = lax.axis_size(axis)
    return lax.ppermute(block, axis, [(i, (i + distance) % size) for i in range(size)])


def split(values):
    high = values.astype(BF16)
    low = (values - high.astype(F32)).astype(BF16)
    return high, low


def start_kernel(*refs):
    sources, outs, places, sem = refs[:7], refs[7:11], refs[11:18], refs[18]
    copies = [pltpu.make_async_copy(src, dst, sem.at[n]) for n, (src, dst) in enumerate(zip(sources, places))]
    for copy in copies:
        copy.start()
    for copy in copies:
        copy.wait()
    prior_ref, obs_ref, start_ref, cells_ref, lengths_ref, kern_ref, noise_ref = places
    shard_ref, gram_ref, prior_out, scale_out = outs
    for slot in range(SPAN):
        lanes = slice(slot * RAYS, (slot + 1) * RAYS)
        base = slot * 2 * TILE
        shard_ref[base:base + TILE, :] = cells_ref[:, lanes].astype(F32)
        shard_ref[base + TILE:base + 2 * TILE, :] = lengths_ref[:, lanes]
    sub = lax.broadcasted_iota(jnp.int32, (8, CHAN), 0)
    kern = jnp.zeros((8, CHAN), F32)
    for s in range(S):
        kern = jnp.where(sub == s, kern_ref[s:s + 1, :], kern)
    weighted = kern * noise_ref[...]
    source = jnp.dot(weighted, obs_ref[...], precision=highest, preferred_element_type=F32)
    base = SPAN * 2 * TILE
    sub = lax.broadcasted_iota(jnp.int32, (8, RAYS), 0)
    start = jnp.broadcast_to(start_ref[...].astype(F32), (8, RAYS))
    shard_ref[base:base + 8, :] = jnp.where(sub == S, start, source)
    wide = jnp.concatenate([kern] * CLAT, axis=0)
    wide_weighted = jnp.concatenate([weighted] * CLAT, axis=0)
    gram = lax.dot_general(wide_weighted, wide, (((1,), (1,)), ((), ())), precision=highest, preferred_element_type=F32)
    row = lax.broadcasted_iota(jnp.int32, gram.shape, 0)
    col = lax.broadcasted_iota(jnp.int32, gram.shape, 1)
    trace = jnp.sum(jnp.where((row == col) & (row < 8), gram, 0.0))
    top = prior_ref[0]
    for s in range(1, S):
        top = jnp.maximum(top, prior_ref[s])
    bound = jnp.full((8, 128), trace * 128.0 + 12.0 * top, F32)
    scale = 1.0 / bound
    scale_out[...] = scale
    gram_ref[...] = jnp.where((row >> 3) == (col >> 3), gram, 0.0) * scale[0:1, 0:1]
    species = lax.broadcasted_iota(jnp.int32, (CLAT * 8, 128), 0) & 7
    prior = jnp.zeros((CLAT * 8, 128), F32)
    for s in range(S):
        prior = jnp.where(species == s, prior_ref[s], prior)
    prior_out[...] = prior * scale[0:1, 0:1]


def gather_kernel(shards, out):
    base = SPAN * 2 * TILE
    for k in range(ORB):
        out[:, k * RAYS:(k + 1) * RAYS] = shards[k, base:base + 8, :]


def build_kernel(shards, w_ref, lat_ref):
    sub = lax.broadcasted_iota(jnp.int32, (8, RAYS), 0)
    odd = (sub & 1) == 1

    def slot_body(index, carry):
        slot, k = index >> 3, index & 7
        spot = pl.multiple_of(k * RAYS, RAYS)
        base = pl.multiple_of(slot * 2 * TILE, 2 * TILE)
        cells = shards[k, pl.ds(base, TILE), :].astype(jnp.int32)
        lengths = shards[k, pl.ds(base + TILE, TILE), :]
        lat_ref[slot, :, pl.ds(spot, RAYS)] = jnp.broadcast_to((cells[0:1, :] >> 7) & 7, (8, RAYS))
        places = ((cells >> 10) << 7) | (cells & 127)
        first = jnp.broadcast_to(cells[0:1, :] & 1, (8, RAYS)) == 1
        swap = first != odd
        keys = []
        sizes = []
        for j in range(TILE // 2):
            even_key = jnp.broadcast_to(places[2 * j:2 * j + 1, :], (8, RAYS))
            odd_key = jnp.broadcast_to(places[2 * j + 1:2 * j + 2, :], (8, RAYS))
            keys.append(jnp.where(swap, odd_key, even_key) - sub)
            even_len = jnp.broadcast_to(lengths[2 * j:2 * j + 1, :], (8, RAYS))
            odd_len = jnp.broadcast_to(lengths[2 * j + 1:2 * j + 2, :], (8, RAYS))
            sizes.append(jnp.where(swap, odd_len, even_len))
        for i in range(TILE // 2):
            for j in range(i + 1, TILE // 2):
                same = keys[i] == keys[j]
                sizes[i] = sizes[i] + jnp.where(same, sizes[j], 0.0)
                keys[j] = jnp.where(same, -64, keys[j])
        for pair in range(CELL // 16):
            parts = []
            for half in range(2):
                offset = pair * 16 + half * 8
                total = jnp.zeros((8, RAYS), F32)
                for key, size in zip(keys, sizes):
                    total = jnp.where(key == offset, size, total)
                parts.append(total)
            high, low = split(jnp.concatenate(parts, axis=0))
            w_ref[slot, pl.ds(pair * 16, 16), pl.ds(spot, RAYS)] = high
            w_ref[slot, pl.ds(CELL + pair * 16, 16), pl.ds(spot, RAYS)] = low
        return carry

    lax.fori_loop(0, SPAN * ORB, slot_body, 0)


def masked_rows(values, lat):
    rows = jnp.concatenate([jnp.where(lat == l, values, 0.0) for l in range(CLAT)], axis=0)
    return jnp.concatenate(split(rows), axis=0)


def back_all(sums, lats, w_ref):
    total = None
    for slot in range(SPAN):
        part = lax.dot_general(
            masked_rows(sums[slot], lats[slot]), w_ref[slot], (((1,), (1,)), ((), ())), preferred_element_type=F32
        )
        total = part if total is None else total + part
    total = total[:, :CELL] + total[:, CELL:]
    return total[:64] + total[64:]


def project_kernel(v_ref, mask_ref, w_ref, own_ref, left_ref, right_ref, left2_ref, right2_ref):
    v = v_ref[...]
    for l in range(CLAT):
        left_ref[4, :, pl.ds(l * LEV, LEV)] = v[8 * l:8 * l + 8, 0:LEV]
        right_ref[4, :, pl.ds(l * LEV, LEV)] = v[8 * l:8 * l + 8, CELL - LEV:]
    halves = jnp.concatenate(split(v), axis=0)
    rows = jnp.concatenate([halves, halves], axis=1)
    for slot in range(SPAN):
        wide = jnp.dot(rows, w_ref[slot], preferred_element_type=F32)
        wide = wide[:64] + wide[64:]
        lat = mask_ref[slot]
        total = jnp.where(lat == 0, wide[0:8], 0.0)
        for l in range(1, CLAT):
            total = total + jnp.where(lat == l, wide[8 * l:8 * l + 8], 0.0)
        own_ref[slot] = total
        if slot >= 1:
            left_ref[slot - 1] = total
        if slot <= 3:
            right_ref[slot] = total
        if slot >= 2:
            left2_ref[slot - 2] = total
        if slot <= 2:
            right2_ref[slot] = total


def init_kernel(z2, z0, z1, z3, z4, lat_ref, w_ref, v_ref, mask_ref, middle_ref, down_ref, up_ref):
    sums, lats = [], []
    sub = lax.broadcasted_iota(jnp.int32, (8, SLOT), 0)
    for slot, z in enumerate((z0, z1, z2, z3, z4)):
        begin = jnp.broadcast_to(z[S:S + 1, :], (8, SLOT))
        present = (begin <= slot) & (begin + (NT - 1) >= slot)
        lat = jnp.where(present, lat_ref[slot], -1)
        mask_ref[slot] = lat
        middle_ref[slot] = jnp.where(begin + 1.0 == slot, 1.0, 0.0)
        lats.append(lat)
        sums.append(jnp.where(sub < S, z[...], 0.0))
    v = back_all(sums, lats, w_ref)
    v_ref[...] = v
    down_ref[...] = v[0:8]
    up_ref[...] = v[56:64]


def ray_sums(own_ref, plus1, minus1, plus2, minus2):
    sums = []
    for slot in range(SPAN):
        total = own_ref[slot]
        if slot <= 3:
            total = total + plus1[slot]
        if slot >= 1:
            total = total + minus1[slot - 1]
        if slot <= 2:
            total = total + plus2[slot]
        if slot >= 2:
            total = total + minus2[slot - 2]
        sums.append(total)
    return sums


def prior_image(v, plus1, minus1, south, north, prior_ref):
    west = jnp.concatenate([minus1[4, :, l * LEV:(l + 1) * LEV] for l in range(CLAT)], axis=0)
    east = jnp.concatenate([plus1[4, :, l * LEV:(l + 1) * LEV] for l in range(CLAT)], axis=0)
    cols = [west] + [v[:, c * LEV:(c + 1) * LEV] for c in range(CLON)] + [east]
    lane = lax.broadcasted_iota(jnp.int32, (64, LEV), 1)
    pieces = []
    for c in range(CLON):
        here = cols[c + 1]
        below = jnp.where(lane == 0, 0.0, pltpu.roll(here, 1, 1))
        above = jnp.where(lane == LEV - 1, 0.0, pltpu.roll(here, LEV - 1, 1))
        south_side = jnp.concatenate([south[:, c * LEV:(c + 1) * LEV], here[:56]], axis=0)
        north_side = jnp.concatenate([here[8:], north[:, c * LEV:(c + 1) * LEV]], axis=0)
        near = cols[c] + cols[c + 2] + below + above + south_side + north_side
        pieces.append(prior_ref[...] * (6.0 * here - near))
    return jnp.concatenate(pieces, axis=1)


def back_image(sums, mask_ref, w_ref, gram_ref):
    image = back_all(sums, [mask_ref[slot] for slot in range(SPAN)], w_ref)
    return jnp.dot(gram_ref[...], image, precision=highest, preferred_element_type=F32)


def back_kernel(v_ref, own_ref, plus1, minus1, plus2, minus2, south, north, mask_ref, w_ref, gram_ref, prior_ref, out_ref, down_ref, up_ref):
    sums = ray_sums(own_ref, plus1, minus1, plus2, minus2)
    v = back_image(sums, mask_ref, w_ref, gram_ref) + prior_image(v_ref[...], plus1, minus1, south, north, prior_ref)
    out_ref[...] = v
    down_ref[...] = v[0:8]
    up_ref[...] = v[56:64]


PAIRS = [(i, j) for i in range(ITERS) for j in range(i, ITERS)] + [(ITERS - 1, ITERS)]


def fold_rows(product):
    product = jnp.sum(product, axis=0, keepdims=True)
    fold = product[:, 0:LEV]
    for c in range(1, product.shape[1] // LEV):
        fold = fold + product[:, c * LEV:(c + 1) * LEV]
    return fold


def sums_kernel(v0, v1, v2, v3, own_ref, plus1, minus1, plus2, minus2, south, north, middle_ref, gram_ref, prior_ref, pair_ref, rays_ref, image_ref):
    sums = ray_sums(own_ref, plus1, minus1, plus2, minus2)
    vectors = [v0[...], v1[...], v2[...], v3[...]]
    image = prior_image(vectors[-1], plus1, minus1, south, north, prior_ref)
    image_ref[...] = image
    last = fold_rows(vectors[-1] * image)
    gram = gram_ref[0:8, 0:8]
    for slot in range(SPAN):
        rays_ref[slot] = sums[slot]
        mixed = jnp.dot(gram, sums[slot], precision=highest, preferred_element_type=F32)
        last = last + fold_rows(sums[slot] * mixed * middle_ref[slot])
    folds = [fold_rows(vectors[i] * vectors[j]) for i, j in PAIRS[:-1]] + [last]
    folds.append(jnp.zeros_like(last))
    folds = [fold + pltpu.roll(fold, LEV // 2, 1) for fold in folds]
    lane = lax.broadcasted_iota(jnp.int32, (1, LEV), 1)
    packed = [jnp.where(lane < LEV // 2, folds[2 * n], folds[2 * n + 1]) for n in range(len(folds) // 2)]
    sub = lax.broadcasted_iota(jnp.int32, (8, LEV), 0)
    block = jnp.zeros((8, LEV), F32)
    for n, row in enumerate(packed):
        block = jnp.where(sub == n, row, block)
    for n in range(pair_ref.shape[0] // 8):
        pair_ref[pl.ds(8 * n, 8), :] = block


def last_kernel(rays_ref, image_ref, mask_ref, w_ref, gram_ref, out_ref):
    sums = [rays_ref[slot] for slot in range(SPAN)]
    out_ref[...] = back_image(sums, mask_ref, w_ref, gram_ref) + image_ref[...]


def combine_kernel(scale_ref, *refs):
    sums_ref, vector_refs, (x_ref, r_ref, spread) = refs[0], refs[1:ITERS + 2], refs[ITERS + 2:]
    parts = [sums_ref[pl.ds(8 * n, 8), :] for n in range(sums_ref.shape[0] // 8)]
    while len(parts) > 1:
        parts = [a + b for a, b in zip(parts[::2], parts[1::2])]
    lane = lax.broadcasted_iota(jnp.int32, (8, LEV), 1)
    lower = jnp.sum(jnp.where(lane < LEV // 2, parts[0], 0.0), axis=1, keepdims=True)
    upper = jnp.sum(jnp.where(lane < LEV // 2, 0.0, parts[0]), axis=1, keepdims=True)
    table = {}
    for n, (i, j) in enumerate(PAIRS):
        half = upper if n & 1 else lower
        table[i, j] = table[j, i] = half[n >> 1:(n >> 1) + 1, :]
    for i in range(ITERS - 1):
        table[i, ITERS] = table[i + 1, ITERS - 1]
    scale = scale_ref[0:1, 0:1]
    zero, one = jnp.zeros((1, 1), F32), jnp.ones((1, 1), F32)
    x = [zero] * (ITERS + 1)
    r = [one] + [zero] * ITERS
    d = list(r)

    def form(a, b, na, nb, off):
        total = None
        for i in range(na):
            inner = None
            for j in range(nb):
                term = b[j] * table[i, j + off]
                inner = term if inner is None else inner + term
            term = a[i] * inner
            total = term if total is None else total + term
        return total

    norm = table[0, 0]
    for k in range(ITERS):
        alpha = norm / form(d, d, k + 1, k + 1, 1)
        for i in range(k + 1):
            x[i] = x[i] + alpha * d[i]
            r[i + 1] = r[i + 1] - alpha * d[i]
        if k < ITERS - 1:
            after = form(r, r, k + 2, k + 2, 0)
            ratio = after / norm
            d = [r[i] + ratio * d[i] for i in range(ITERS + 1)]
            norm = after
    x = [scale * value for value in x]
    for c in range(CLON):
        parts = [ref[:, c * LEV:(c + 1) * LEV] for ref in vector_refs]
        total = x[0] * parts[0]
        for i in range(1, ITERS):
            total = total + x[i] * parts[i]
        spread[0, c] = total
        total = r[0] * parts[0]
        for i in range(1, ITERS + 1):
            total = total + r[i] * parts[i]
        spread[1, c] = total
        for s in range(S):
            x_ref[s, c] = spread[0, c, pl.ds(s, CLAT, stride=8), :]
            r_ref[s, c] = spread[1, c, pl.ds(s, CLAT, stride=8), :]


def shape(*dims, dtype=F32):
    return jax.ShapeDtypeStruct(dims, dtype)


def call(kernel, outs, n_in, scalar=False, scratch=(), work=None):
    return pl.pallas_call(
        kernel,
        out_shape=outs,
        in_specs=([sspec()] if scalar else []) + [vspec()] * n_in,
        out_specs=[vspec()] * len(outs),
        scratch_shapes=scratch,
        compiler_params=LIMIT,
        cost_estimate=work,
    )


MATMUL = pl.CostEstimate(flops=2 * 128 * 2 * CELL * SPAN * SLOT, transcendentals=0, bytes_accessed=2 * 2 * CELL * SPAN * SLOT)
BUILD = pl.CostEstimate(flops=16 * TILE * CELL * SPAN * SLOT, transcendentals=0, bytes_accessed=4 * 2 * CELL * SPAN * SLOT)
MESSAGES = (shape(SPAN, 8, SLOT), shape(5, 8, SLOT), shape(5, 8, SLOT), shape(3, 8, SLOT), shape(3, 8, SLOT))
FACE = shape(8, CELL)
FIELD = shape(64, CELL)


def lat_faces(down, up):
    n_lat = lax.axis_size("lat")
    south = lax.ppermute(up, "lat", [(i, i + 1) for i in range(n_lat - 1)])
    north = lax.ppermute(down, "lat", [(i + 1, i) for i in range(n_lat - 1)])
    return south, north


def exchange(south, north, own, left, right, left2, right2):
    south, north, left, right, left2, right2 = lax.optimization_barrier((south, north, left, right, left2, right2))
    plus2 = shift(left2, "lon", -2)
    minus2 = shift(right2, "lon", 2)
    plus1 = shift(left, "lon", -1)
    minus1 = shift(right, "lon", 1)
    return own, plus1, minus1, plus2, minus2, south, north


def body(observed, ray_start, tile_cells, tile_lengths, channel_kernel, noise_weight, prior_weight):
    shard, gram, prior, scale = pl.pallas_call(
        start_kernel,
        out_shape=(shape(SHARD, RAYS), shape(64, 64), shape(64, LEV), shape(8, LEV)),
        in_specs=[pl.BlockSpec(memory_space=pltpu.HBM)] * 7,
        out_specs=[vspec()] * 4,
        scratch_shapes=[
            pltpu.SMEM((S,), F32),
            pltpu.VMEM((CHAN, RAYS), F32),
            pltpu.VMEM((1, RAYS), jnp.int32),
            pltpu.VMEM((TILE, SPAN * RAYS), jnp.int32),
            pltpu.VMEM((TILE, SPAN * RAYS), F32),
            pltpu.VMEM((S, CHAN), F32),
            pltpu.VMEM((1, CHAN), F32),
            pltpu.SemaphoreType.DMA((7,)),
        ],
        compiler_params=LIMIT,
    )(prior_weight, observed.T, ray_start.reshape(1, RAYS), tile_cells.T, tile_lengths.T, channel_kernel, noise_weight.reshape(1, -1))
    shards = lax.all_gather(shard, "orbit")
    (z,) = call(gather_kernel, (shape(8, SLOT),), 1)(shards)
    z1, z3 = shift(z, "lon", -1), shift(z, "lon", 1)
    z0, z4 = shift(z, "lon", -2), shift(z, "lon", 2)
    w, lat = call(build_kernel, (shape(SPAN, 2 * CELL, SLOT, dtype=BF16), shape(SPAN, 8, SLOT, dtype=jnp.int32)), 1, work=BUILD)(shards)
    mask_shape = shape(SPAN, 8, SLOT, dtype=jnp.int32)
    v, mask, middle, down, up = call(init_kernel, (FIELD, mask_shape, shape(SPAN, 8, SLOT), FACE, FACE), 7, work=MATMUL)(z, z0, z1, z3, z4, lat, w)
    south, north = lat_faces(down, up)
    vectors = [v]
    sent = call(project_kernel, MESSAGES, 3, work=MATMUL)(v, mask, w)
    for turn in range(ITERS - 1):
        received = exchange(south, north, *sent)
        v, down, up = call(back_kernel, (FIELD, FACE, FACE), 12, work=MATMUL)(v, *received, mask, w, gram, prior)
        south, north = lat_faces(down, up)
        vectors.append(v)
        sent = call(project_kernel, MESSAGES, 3, work=MATMUL)(v, mask, w)
    peers = lax.axis_size("lon") * lax.axis_size("lat")
    pairs, rays, image = call(sums_kernel, (shape(8 * peers, LEV), shape(SPAN, 8, SLOT), FIELD), 14)(
        *vectors, *exchange(south, north, *sent), middle, gram, prior
    )
    pairs = lax.all_to_all(pairs, ("lon", "lat"), 0, 0, tiled=True)
    (v,) = call(last_kernel, (FIELD,), 5, work=MATMUL)(rays, image, mask, w, gram)
    vectors.append(v)
    field = shape(S, CLON, CLAT, LEV)
    return tuple(call(combine_kernel, (field, field), ITERS + 3, False, [pltpu.VMEM((2, CLON, 64, LEV), F32)])(scale, pairs, *vectors))


def solution(mesh):
    return jax.shard_map(
        body,
        mesh=mesh,
        in_specs=(
            P(("orbit", "lon", "lat"), None),
            P(("orbit", "lon", "lat")),
            P(("orbit", "lon", "lat"), None),
            P(("orbit", "lon", "lat"), None),
            P(),
            P(),
            P(),
        ),
        out_specs=(P(None, "lon", "lat", None), P(None, "lon", "lat", None)),
        check_vma=False,
    )
```

```python
import jax
import jax.numpy as jnp
from jax import lax
from jax.experimental import pallas as pl
from jax.experimental.pallas import tpu as pltpu
from jax.sharding import PartitionSpec as P

S = 7
CLON = 4
CLAT = 8
LEV = 128
NT = 3
TILE = 16
ITERS = 4
SPAN = 5
ORB = 8
RAYS = 128
SLOT = ORB * RAYS
CELL = CLON * LEV
CHAN = 64
SHARD = SPAN * 2 * TILE + 8
F32 = jnp.float32
BF16 = jnp.bfloat16
highest = lax.Precision.HIGHEST
VMEM = pltpu.VMEM
LIMIT = pltpu.CompilerParams(vmem_limit_bytes=24 << 20)


def vspec():
    return pl.BlockSpec(memory_space=pltpu.VMEM)


def sspec():
    return pl.BlockSpec(memory_space=pltpu.SMEM)


def shift(block, axis, distance):
    size = lax.axis_size(axis)
    return lax.ppermute(block, axis, [(i, (i + distance) % size) for i in range(size)])


def split(values):
    high = values.astype(BF16)
    low = (values - high.astype(F32)).astype(BF16)
    return high, low


def start_kernel(*refs):
    sources, outs, places, sem = refs[:7], refs[7:11], refs[11:18], refs[18]
    copies = [pltpu.make_async_copy(src, dst, sem.at[n]) for n, (src, dst) in enumerate(zip(sources, places))]
    for copy in copies:
        copy.start()
    for copy in copies:
        copy.wait()
    prior_ref, obs_ref, start_ref, cells_ref, lengths_ref, kern_ref, noise_ref = places
    shard_ref, gram_ref, prior_out, scale_out = outs
    for slot in range(SPAN):
        lanes = slice(slot * RAYS, (slot + 1) * RAYS)
        base = slot * 2 * TILE
        shard_ref[base:base + TILE, :] = cells_ref[:, lanes].astype(F32)
        shard_ref[base + TILE:base + 2 * TILE, :] = lengths_ref[:, lanes]
    sub = lax.broadcasted_iota(jnp.int32, (8, CHAN), 0)
    kern = jnp.zeros((8, CHAN), F32)
    for s in range(S):
        kern = jnp.where(sub == s, kern_ref[s:s + 1, :], kern)
    weighted = kern * noise_ref[...]
    source = jnp.dot(weighted, obs_ref[...], precision=highest, preferred_element_type=F32)
    base = SPAN * 2 * TILE
    sub = lax.broadcasted_iota(jnp.int32, (8, RAYS), 0)
    start = jnp.broadcast_to(start_ref[...].astype(F32), (8, RAYS))
    shard_ref[base:base + 8, :] = jnp.where(sub == S, start, source)
    wide = jnp.concatenate([kern] * CLAT, axis=0)
    wide_weighted = jnp.concatenate([weighted] * CLAT, axis=0)
    gram = lax.dot_general(wide_weighted, wide, (((1,), (1,)), ((), ())), precision=highest, preferred_element_type=F32)
    row = lax.broadcasted_iota(jnp.int32, gram.shape, 0)
    col = lax.broadcasted_iota(jnp.int32, gram.shape, 1)
    trace = jnp.sum(jnp.where((row == col) & (row < 8), gram, 0.0))
    top = prior_ref[0]
    for s in range(1, S):
        top = jnp.maximum(top, prior_ref[s])
    bound = jnp.full((8, 128), trace * 128.0 + 12.0 * top, F32)
    scale = 1.0 / bound
    scale_out[...] = scale
    gram_ref[...] = jnp.where((row >> 3) == (col >> 3), gram, 0.0) * scale[0:1, 0:1]
    species = lax.broadcasted_iota(jnp.int32, (CLAT * 8, 128), 0) & 7
    prior = jnp.zeros((CLAT * 8, 128), F32)
    for s in range(S):
        prior = jnp.where(species == s, prior_ref[s], prior)
    prior_out[...] = prior * scale[0:1, 0:1]


def gather_kernel(shards, out):
    base = SPAN * 2 * TILE
    for k in range(ORB):
        out[:, k * RAYS:(k + 1) * RAYS] = shards[k, base:base + 8, :]


def build_kernel(shards, w_ref, lat_ref):
    sub = lax.broadcasted_iota(jnp.int32, (8, RAYS), 0)
    odd = (sub & 1) == 1

    def slot_body(index, carry):
        slot, k = index >> 3, index & 7
        spot = pl.multiple_of(k * RAYS, RAYS)
        base = pl.multiple_of(slot * 2 * TILE, 2 * TILE)
        cells = shards[k, pl.ds(base, TILE), :].astype(jnp.int32)
        lengths = shards[k, pl.ds(base + TILE, TILE), :]
        lat_ref[slot, :, pl.ds(spot, RAYS)] = jnp.broadcast_to((cells[0:1, :] >> 7) & 7, (8, RAYS))
        places = ((cells >> 10) << 7) | (cells & 127)
        first = jnp.broadcast_to(cells[0:1, :] & 1, (8, RAYS)) == 1
        swap = first != odd
        keys = []
        sizes = []
        for j in range(TILE // 2):
            even_key = jnp.broadcast_to(places[2 * j:2 * j + 1, :], (8, RAYS))
            odd_key = jnp.broadcast_to(places[2 * j + 1:2 * j + 2, :], (8, RAYS))
            keys.append(jnp.where(swap, odd_key, even_key) - sub)
            even_len = jnp.broadcast_to(lengths[2 * j:2 * j + 1, :], (8, RAYS))
            odd_len = jnp.broadcast_to(lengths[2 * j + 1:2 * j + 2, :], (8, RAYS))
            sizes.append(jnp.where(swap, odd_len, even_len))
        for i in range(TILE // 2):
            for j in range(i + 1, TILE // 2):
                same = keys[i] == keys[j]
                sizes[i] = sizes[i] + jnp.where(same, sizes[j], 0.0)
                keys[j] = jnp.where(same, -64, keys[j])
        for pair in range(CELL // 16):
            parts = []
            for half in range(2):
                offset = pair * 16 + half * 8
                total = jnp.zeros((8, RAYS), F32)
                for key, size in zip(keys, sizes):
                    total = jnp.where(key == offset, size, total)
                parts.append(total)
            high, low = split(jnp.concatenate(parts, axis=0))
            w_ref[slot, pl.ds(pair * 16, 16), pl.ds(spot, RAYS)] = high
            w_ref[slot, pl.ds(CELL + pair * 16, 16), pl.ds(spot, RAYS)] = low
        return carry

    lax.fori_loop(0, SPAN * ORB, slot_body, 0)


def masked_rows(values, lat):
    rows = jnp.concatenate([jnp.where(lat == l, values, 0.0) for l in range(CLAT)], axis=0)
    return jnp.concatenate(split(rows), axis=0)


def back_all(sums, lats, w_ref):
    total = None
    for slot in range(SPAN):
        part = lax.dot_general(
            w_ref[slot], masked_rows(sums[slot], lats[slot]), (((1,), (1,)), ((), ())), preferred_element_type=F32
        )
        total = part if total is None else total + part
    total = (total[:CELL] + total[CELL:]).T
    return total[:64] + total[64:]


def project_all(v, lats, w_ref, outs):
    own_ref, left_ref, right_ref, left2_ref, right2_ref, down_ref, up_ref = outs
    down_ref[...] = v[0:8]
    up_ref[...] = v[56:64]
    for l in range(CLAT):
        left_ref[4, :, pl.ds(l * LEV, LEV)] = v[8 * l:8 * l + 8, 0:LEV]
        right_ref[4, :, pl.ds(l * LEV, LEV)] = v[8 * l:8 * l + 8, CELL - LEV:]
    halves = jnp.concatenate(split(v), axis=0)
    rows = jnp.concatenate([halves, halves], axis=1)
    for slot in range(SPAN):
        wide = jnp.dot(rows, w_ref[slot], preferred_element_type=F32)
        wide = wide[:64] + wide[64:]
        lat = lats[slot]
        total = jnp.where(lat == 0, wide[0:8], 0.0)
        for l in range(1, CLAT):
            total = total + jnp.where(lat == l, wide[8 * l:8 * l + 8], 0.0)
        own_ref[slot] = total
        if slot >= 1:
            left_ref[slot - 1] = total
        if slot <= 3:
            right_ref[slot] = total
        if slot >= 2:
            left2_ref[slot - 2] = total
        if slot <= 2:
            right2_ref[slot] = total


def init_kernel(z2, z0, z1, z3, z4, lat_ref, w_ref, v_ref, mask_ref, *outs):
    sums, lats = [], []
    sub = lax.broadcasted_iota(jnp.int32, (8, SLOT), 0)
    for slot, z in enumerate((z0, z1, z2, z3, z4)):
        begin = jnp.broadcast_to(z[S:S + 1, :], (8, SLOT))
        present = (begin <= slot) & (begin + (NT - 1) >= slot)
        lat = jnp.where(present, lat_ref[slot], -1)
        mask_ref[slot] = lat
        lats.append(lat)
        sums.append(jnp.where(sub < S, z[...], 0.0))
    v = back_all(sums, lats, w_ref)
    v_ref[...] = v
    project_all(v, lats, w_ref, outs)


def ray_sums(own_ref, plus1, minus1, plus2, minus2):
    sums = []
    for slot in range(SPAN):
        total = own_ref[slot]
        if slot <= 3:
            total = total + plus1[slot]
        if slot >= 1:
            total = total + minus1[slot - 1]
        if slot <= 2:
            total = total + plus2[slot]
        if slot >= 2:
            total = total + minus2[slot - 2]
        sums.append(total)
    return sums


def prior_image(v, plus1, minus1, south, north, prior_ref):
    west = jnp.concatenate([minus1[4, :, l * LEV:(l + 1) * LEV] for l in range(CLAT)], axis=0)
    east = jnp.concatenate([plus1[4, :, l * LEV:(l + 1) * LEV] for l in range(CLAT)], axis=0)
    cols = [west] + [v[:, c * LEV:(c + 1) * LEV] for c in range(CLON)] + [east]
    lane = lax.broadcasted_iota(jnp.int32, (64, LEV), 1)
    pieces = []
    for c in range(CLON):
        here = cols[c + 1]
        below = jnp.where(lane == 0, 0.0, pltpu.roll(here, 1, 1))
        above = jnp.where(lane == LEV - 1, 0.0, pltpu.roll(here, LEV - 1, 1))
        south_side = jnp.concatenate([south[:, c * LEV:(c + 1) * LEV], here[:56]], axis=0)
        north_side = jnp.concatenate([here[8:], north[:, c * LEV:(c + 1) * LEV]], axis=0)
        near = cols[c] + cols[c + 2] + below + above + south_side + north_side
        pieces.append(prior_ref[...] * (6.0 * here - near))
    return jnp.concatenate(pieces, axis=1)


def next_vector(v_ref, own_ref, plus1, minus1, plus2, minus2, south, north, lats, w_ref, gram_ref, prior_ref):
    image = back_all(ray_sums(own_ref, plus1, minus1, plus2, minus2), lats, w_ref)
    image = jnp.dot(gram_ref[...], image, precision=highest, preferred_element_type=F32)
    return image + prior_image(v_ref[...], plus1, minus1, south, north, prior_ref)


def step_kernel(*refs):
    lats = [refs[8][slot] for slot in range(SPAN)]
    v = next_vector(*refs[:8], lats, *refs[9:12])
    refs[12][...] = v
    project_all(v, lats, refs[9], refs[13:])


PAIRS = [(i, j) for i in range(ITERS) for j in range(i, ITERS)] + [(ITERS - 1, ITERS)]


def last_kernel(*refs):
    lats = [refs[8][slot] for slot in range(SPAN)]
    v = next_vector(*refs[:8], lats, *refs[9:12])
    earlier, (out_ref, pair_ref) = refs[12:12 + ITERS - 1], refs[12 + ITERS - 1:]
    out_ref[...] = v
    vectors = [ref[...] for ref in earlier] + [refs[0][...], v]
    lane = lax.broadcasted_iota(jnp.int32, (1, LEV), 1)
    row = jnp.zeros((1, LEV), F32)
    for n, (i, j) in enumerate(PAIRS):
        product = jnp.sum(vectors[i] * vectors[j], axis=0, keepdims=True)
        row = jnp.where(lane == n, jnp.sum(product, axis=1, keepdims=True), row)
    pair_ref[...] = jnp.broadcast_to(row, pair_ref.shape)


def combine_kernel(scale_ref, *refs):
    sums_ref, vector_refs, (x_ref, r_ref, spread) = refs[0], refs[1:ITERS + 2], refs[ITERS + 2:]
    row = jnp.sum(sums_ref[...], axis=0, keepdims=True)
    table = {}
    for n, (i, j) in enumerate(PAIRS):
        table[i, j] = table[j, i] = row[:, n:n + 1]
    for i in range(ITERS - 1):
        table[i, ITERS] = table[i + 1, ITERS - 1]
    scale = scale_ref[0:1, 0:1]
    zero, one = jnp.zeros((1, 1), F32), jnp.ones((1, 1), F32)
    x = [zero] * (ITERS + 1)
    r = [one] + [zero] * ITERS
    d = list(r)

    def form(a, b, na, nb, off):
        total = None
        for i in range(na):
            inner = None
            for j in range(nb):
                term = b[j] * table[i, j + off]
                inner = term if inner is None else inner + term
            term = a[i] * inner
            total = term if total is None else total + term
        return total

    norm = table[0, 0]
    for k in range(ITERS):
        alpha = norm / form(d, d, k + 1, k + 1, 1)
        for i in range(k + 1):
            x[i] = x[i] + alpha * d[i]
            r[i + 1] = r[i + 1] - alpha * d[i]
        if k < ITERS - 1:
            after = form(r, r, k + 2, k + 2, 0)
            ratio = after / norm
            d = [r[i] + ratio * d[i] for i in range(ITERS + 1)]
            norm = after
    x = [scale * value for value in x]
    for c in range(CLON):
        parts = [ref[:, c * LEV:(c + 1) * LEV] for ref in vector_refs]
        total = x[0] * parts[0]
        for i in range(1, ITERS):
            total = total + x[i] * parts[i]
        spread[0, c] = total
        total = r[0] * parts[0]
        for i in range(1, ITERS + 1):
            total = total + r[i] * parts[i]
        spread[1, c] = total
        for s in range(S):
            x_ref[s, c] = spread[0, c, pl.ds(s, CLAT, stride=8), :]
            r_ref[s, c] = spread[1, c, pl.ds(s, CLAT, stride=8), :]


def shape(*dims, dtype=F32):
    return jax.ShapeDtypeStruct(dims, dtype)


def call(kernel, outs, n_in, scalar=False, scratch=(), work=None):
    return pl.pallas_call(
        kernel,
        out_shape=outs,
        in_specs=([sspec()] if scalar else []) + [vspec()] * n_in,
        out_specs=[vspec()] * len(outs),
        scratch_shapes=scratch,
        compiler_params=LIMIT,
        cost_estimate=work,
    )


MATMUL = pl.CostEstimate(flops=2 * 128 * 2 * CELL * SPAN * SLOT, transcendentals=0, bytes_accessed=2 * 2 * CELL * SPAN * SLOT)
BUILD = pl.CostEstimate(flops=16 * TILE * CELL * SPAN * SLOT, transcendentals=0, bytes_accessed=4 * 2 * CELL * SPAN * SLOT)
MESSAGES = (shape(SPAN, 8, SLOT), shape(5, 8, SLOT), shape(5, 8, SLOT), shape(3, 8, SLOT), shape(3, 8, SLOT))
FACE = shape(8, CELL)
FIELD = shape(64, CELL)
SENT = MESSAGES + (FACE, FACE)


def exchange(own, left, right, left2, right2, down, up):
    n_lat = lax.axis_size("lat")
    plus1 = shift(left, "lon", -1)
    minus1 = shift(right, "lon", 1)
    plus2 = shift(left2, "lon", -2)
    minus2 = shift(right2, "lon", 2)
    south = lax.ppermute(up, "lat", [(i, i + 1) for i in range(n_lat - 1)])
    plus1, down = lax.optimization_barrier((plus1, down))
    north = lax.ppermute(down, "lat", [(i + 1, i) for i in range(n_lat - 1)])
    return own, plus1, minus1, plus2, minus2, south, north


def body(observed, ray_start, tile_cells, tile_lengths, channel_kernel, noise_weight, prior_weight):
    shard, gram, prior, scale = pl.pallas_call(
        start_kernel,
        out_shape=(shape(SHARD, RAYS), shape(64, 64), shape(64, LEV), shape(8, LEV)),
        in_specs=[pl.BlockSpec(memory_space=pltpu.HBM)] * 7,
        out_specs=[vspec()] * 4,
        scratch_shapes=[
            pltpu.SMEM((S,), F32),
            pltpu.VMEM((CHAN, RAYS), F32),
            pltpu.VMEM((1, RAYS), jnp.int32),
            pltpu.VMEM((TILE, SPAN * RAYS), jnp.int32),
            pltpu.VMEM((TILE, SPAN * RAYS), F32),
            pltpu.VMEM((S, CHAN), F32),
            pltpu.VMEM((1, CHAN), F32),
            pltpu.SemaphoreType.DMA((7,)),
        ],
        compiler_params=LIMIT,
    )(*[
        pltpu.with_memory_space_constraint(value, pltpu.HBM)
        for value in (prior_weight, observed.T, ray_start.reshape(1, RAYS), tile_cells.T, tile_lengths.T, channel_kernel, noise_weight.reshape(1, -1))
    ])
    shards = lax.all_gather(shard, "orbit")
    (z,) = call(gather_kernel, (shape(8, SLOT),), 1)(shards)
    z1, z3 = shift(z, "lon", -1), shift(z, "lon", 1)
    z0, z4 = shift(z, "lon", -2), shift(z, "lon", 2)
    w, lat = call(build_kernel, (shape(SPAN, 2 * CELL, SLOT, dtype=BF16), shape(SPAN, 8, SLOT, dtype=jnp.int32)), 1, work=BUILD)(shards)
    mask_shape = shape(SPAN, 8, SLOT, dtype=jnp.int32)
    v, mask, *sent = call(init_kernel, (FIELD, mask_shape) + SENT, 7, work=MATMUL)(z, z0, z1, z3, z4, lat, w)
    vectors = [v]
    for turn in range(ITERS - 1):
        v, *sent = call(step_kernel, (FIELD,) + SENT, 12, work=MATMUL)(v, *exchange(*sent), mask, w, gram, prior)
        vectors.append(v)
    peers = lax.axis_size("lon") * lax.axis_size("lat")
    v, pairs = call(last_kernel, (FIELD, shape(peers, LEV)), 12 + ITERS - 1, work=MATMUL)(
        v, *exchange(*sent), mask, w, gram, prior, *vectors[:-1]
    )
    vectors.append(v)
    pairs = lax.all_to_all(pairs, ("lon", "lat"), 0, 0, tiled=True)
    field = shape(S, CLON, CLAT, LEV)
    return tuple(call(combine_kernel, (field, field), ITERS + 3, False, [pltpu.VMEM((2, CLON, 64, LEV), F32)])(scale, pairs, *vectors))


def solution(mesh):
    return jax.shard_map(
        body,
        mesh=mesh,
        in_specs=(
            P(("orbit", "lon", "lat"), None),
            P(("orbit", "lon", "lat")),
            P(("orbit", "lon", "lat"), None),
            P(("orbit", "lon", "lat"), None),
            P(),
            P(),
            P(),
        ),
        out_specs=(P(None, "lon", "lat", None), P(None, "lon", "lat", None)),
        check_vma=False,
    )
```

```python
import jax
import jax.numpy as jnp
from jax import lax
from jax.experimental import pallas as pl
from jax.experimental.pallas import tpu as pltpu
from jax.sharding import PartitionSpec as P

S = 7
CLON = 4
CLAT = 8
LEV = 128
NT = 3
TILE = 16
ITERS = 4
SPAN = 5
ORB = 8
RAYS = 128
SLOT = ORB * RAYS
CELL = CLON * LEV
CHAN = 64
TABLE = SPAN * 2 * TILE
F32 = jnp.float32
BF16 = jnp.bfloat16
highest = lax.Precision.HIGHEST
VMEM = pltpu.VMEM
LIMIT = pltpu.CompilerParams(vmem_limit_bytes=24 << 20)


def vspec():
    return pl.BlockSpec(memory_space=pltpu.VMEM)


def sspec():
    return pl.BlockSpec(memory_space=pltpu.SMEM)


def shift(block, axis, distance):
    size = lax.axis_size(axis)
    return lax.ppermute(block, axis, [(i, (i + distance) % size) for i in range(size)])


def split(values):
    high = values.astype(BF16)
    low = (values - high.astype(F32)).astype(BF16)
    return high, low


def fetch(sources, places, sem):
    copies = [pltpu.make_async_copy(src, dst, sem.at[n]) for n, (src, dst) in enumerate(zip(sources, places))]
    for copy in copies:
        copy.start()
    for copy in copies:
        copy.wait()


def source_kernel(*refs):
    sources, source_ref, places, sem = refs[:4], refs[4], refs[5:9], refs[9]
    fetch(sources, places, sem)
    obs_ref, start_ref, kern_ref, noise_ref = places
    kern = species_rows(kern_ref)
    source = jnp.dot(kern * noise_ref[...], obs_ref[...], precision=highest, preferred_element_type=F32)
    sub = lax.broadcasted_iota(jnp.int32, (8, RAYS), 0)
    start = jnp.broadcast_to(start_ref[...].astype(F32), (8, RAYS))
    source_ref[...] = jnp.where(sub == S, start, source)


def species_rows(kern_ref):
    sub = lax.broadcasted_iota(jnp.int32, (8, CHAN), 0)
    kern = jnp.zeros((8, CHAN), F32)
    for s in range(S):
        kern = jnp.where(sub == s, kern_ref[s:s + 1, :], kern)
    return kern


def table_kernel(*refs):
    sources, outs, places, sem = refs[:5], refs[5:9], refs[9:14], refs[14]
    fetch(sources, places, sem)
    prior_ref, cells_ref, lengths_ref, kern_ref, noise_ref = places
    table_ref, gram_ref, prior_out, scale_out = outs
    for slot in range(SPAN):
        lanes = slice(slot * RAYS, (slot + 1) * RAYS)
        base = slot * 2 * TILE
        table_ref[base:base + TILE, :] = cells_ref[:, lanes].astype(F32)
        table_ref[base + TILE:base + 2 * TILE, :] = lengths_ref[:, lanes]
    kern = species_rows(kern_ref)
    weighted = kern * noise_ref[...]
    wide = jnp.concatenate([kern] * CLAT, axis=0)
    wide_weighted = jnp.concatenate([weighted] * CLAT, axis=0)
    gram = lax.dot_general(wide_weighted, wide, (((1,), (1,)), ((), ())), precision=highest, preferred_element_type=F32)
    row = lax.broadcasted_iota(jnp.int32, gram.shape, 0)
    col = lax.broadcasted_iota(jnp.int32, gram.shape, 1)
    trace = jnp.sum(jnp.where((row == col) & (row < 8), gram, 0.0))
    top = prior_ref[0]
    for s in range(1, S):
        top = jnp.maximum(top, prior_ref[s])
    bound = jnp.full((8, 128), trace * 128.0 + 12.0 * top, F32)
    scale = 1.0 / bound
    scale_out[...] = scale
    gram_ref[...] = jnp.where((row >> 3) == (col >> 3), gram, 0.0) * scale[0:1, 0:1]
    species = lax.broadcasted_iota(jnp.int32, (CLAT * 8, 128), 0) & 7
    prior = jnp.zeros((CLAT * 8, 128), F32)
    for s in range(S):
        prior = jnp.where(species == s, prior_ref[s], prior)
    prior_out[...] = prior * scale[0:1, 0:1]


def build_kernel(shards, w_ref, lat_ref):
    sub = lax.broadcasted_iota(jnp.int32, (8, RAYS), 0)
    odd = (sub & 1) == 1

    def slot_body(index, carry):
        slot, k = index >> 3, index & 7
        spot = pl.multiple_of(k * RAYS, RAYS)
        base = pl.multiple_of(slot * 2 * TILE, 2 * TILE)
        cells = shards[k, pl.ds(base, TILE), :].astype(jnp.int32)
        lengths = shards[k, pl.ds(base + TILE, TILE), :]
        lat_ref[slot, :, pl.ds(spot, RAYS)] = jnp.broadcast_to((cells[0:1, :] >> 7) & 7, (8, RAYS))
        places = ((cells >> 10) << 7) | (cells & 127)
        first = jnp.broadcast_to(cells[0:1, :] & 1, (8, RAYS)) == 1
        swap = first != odd
        keys = []
        sizes = []
        for j in range(TILE // 2):
            even_key = jnp.broadcast_to(places[2 * j:2 * j + 1, :], (8, RAYS))
            odd_key = jnp.broadcast_to(places[2 * j + 1:2 * j + 2, :], (8, RAYS))
            keys.append(jnp.where(swap, odd_key, even_key) - sub)
            even_len = jnp.broadcast_to(lengths[2 * j:2 * j + 1, :], (8, RAYS))
            odd_len = jnp.broadcast_to(lengths[2 * j + 1:2 * j + 2, :], (8, RAYS))
            sizes.append(jnp.where(swap, odd_len, even_len))
        for i in range(TILE // 2):
            for j in range(i + 1, TILE // 2):
                same = keys[i] == keys[j]
                sizes[i] = sizes[i] + jnp.where(same, sizes[j], 0.0)
                keys[j] = jnp.where(same, -64, keys[j])
        for pair in range(CELL // 16):
            parts = []
            for half in range(2):
                offset = pair * 16 + half * 8
                total = jnp.zeros((8, RAYS), F32)
                for key, size in zip(keys, sizes):
                    total = jnp.where(key == offset, size, total)
                parts.append(total)
            high, low = split(jnp.concatenate(parts, axis=0))
            w_ref[slot, pl.ds(pair * 16, 16), pl.ds(spot, RAYS)] = high
            w_ref[slot, pl.ds(CELL + pair * 16, 16), pl.ds(spot, RAYS)] = low
        return carry

    lax.fori_loop(0, SPAN * ORB, slot_body, 0)


def masked_rows(values, lat):
    rows = jnp.concatenate([jnp.where(lat == l, values, 0.0) for l in range(CLAT)], axis=0)
    return jnp.concatenate(split(rows), axis=0)


def back_all(sums, lats, w_ref):
    total = None
    for slot in range(SPAN):
        part = lax.dot_general(
            w_ref[slot], masked_rows(sums[slot], lats[slot]), (((1,), (1,)), ((), ())), preferred_element_type=F32
        )
        total = part if total is None else total + part
    total = (total[:CELL] + total[CELL:]).T
    return total[:64] + total[64:]


def project_kernel(v_ref, mask_ref, w_ref, own_ref, left_ref, right_ref, left2_ref, right2_ref, down_ref, up_ref):
    v = v_ref[...]
    down_ref[...] = v[0:8]
    up_ref[...] = v[56:64]
    for l in range(CLAT):
        left_ref[4, :, pl.ds(l * LEV, LEV)] = v[8 * l:8 * l + 8, 0:LEV]
        right_ref[4, :, pl.ds(l * LEV, LEV)] = v[8 * l:8 * l + 8, CELL - LEV:]
    halves = jnp.concatenate(split(v), axis=0)
    rows = jnp.concatenate([halves, halves], axis=1)
    for slot in range(SPAN):
        wide = jnp.dot(rows, w_ref[slot], preferred_element_type=F32)
        wide = wide[:64] + wide[64:]
        lat = mask_ref[slot]
        total = jnp.where(lat == 0, wide[0:8], 0.0)
        for l in range(1, CLAT):
            total = total + jnp.where(lat == l, wide[8 * l:8 * l + 8], 0.0)
        own_ref[slot] = total
        if slot >= 1:
            left_ref[slot - 1] = total
        if slot <= 3:
            right_ref[slot] = total
        if slot >= 2:
            left2_ref[slot - 2] = total
        if slot <= 2:
            right2_ref[slot] = total


def init_kernel(shards, lat_ref, w_ref, v_ref, mask_ref):
    sums, lats = [], []
    sub = lax.broadcasted_iota(jnp.int32, (8, SLOT), 0)
    for slot in range(SPAN):
        base = TABLE + 8 * slot
        z = jnp.concatenate([shards[k, base:base + 8, :] for k in range(ORB)], axis=1)
        begin = jnp.broadcast_to(z[S:S + 1, :], (8, SLOT))
        present = (begin <= slot) & (begin + (NT - 1) >= slot)
        lat = jnp.where(present, lat_ref[slot], -1)
        mask_ref[slot] = lat
        lats.append(lat)
        sums.append(jnp.where(sub < S, z, 0.0))
    v_ref[...] = back_all(sums, lats, w_ref)


def ray_sums(own_ref, plus1, minus1, plus2, minus2):
    sums = []
    for slot in range(SPAN):
        total = own_ref[slot]
        if slot <= 3:
            total = total + plus1[slot]
        if slot >= 1:
            total = total + minus1[slot - 1]
        if slot <= 2:
            total = total + plus2[slot]
        if slot >= 2:
            total = total + minus2[slot - 2]
        sums.append(total)
    return sums


def prior_image(v, plus1, minus1, south, north, prior_ref):
    west = jnp.concatenate([minus1[4, :, l * LEV:(l + 1) * LEV] for l in range(CLAT)], axis=0)
    east = jnp.concatenate([plus1[4, :, l * LEV:(l + 1) * LEV] for l in range(CLAT)], axis=0)
    cols = [west] + [v[:, c * LEV:(c + 1) * LEV] for c in range(CLON)] + [east]
    lane = lax.broadcasted_iota(jnp.int32, (64, LEV), 1)
    pieces = []
    for c in range(CLON):
        here = cols[c + 1]
        below = jnp.where(lane == 0, 0.0, pltpu.roll(here, 1, 1))
        above = jnp.where(lane == LEV - 1, 0.0, pltpu.roll(here, LEV - 1, 1))
        south_side = jnp.concatenate([south[:, c * LEV:(c + 1) * LEV], here[:56]], axis=0)
        north_side = jnp.concatenate([here[8:], north[:, c * LEV:(c + 1) * LEV]], axis=0)
        near = cols[c] + cols[c + 2] + below + above + south_side + north_side
        pieces.append(prior_ref[...] * (6.0 * here - near))
    return jnp.concatenate(pieces, axis=1)


def next_vector(v_ref, own_ref, plus1, minus1, plus2, minus2, south, north, lats, w_ref, gram_ref, prior_ref):
    image = back_all(ray_sums(own_ref, plus1, minus1, plus2, minus2), lats, w_ref)
    image = jnp.dot(gram_ref[...], image, precision=highest, preferred_element_type=F32)
    return image + prior_image(v_ref[...], plus1, minus1, south, north, prior_ref)


def step_kernel(*refs):
    lats = [refs[8][slot] for slot in range(SPAN)]
    refs[12][...] = next_vector(*refs[:8], lats, *refs[9:12])


PAIRS = [(i, j) for i in range(ITERS) for j in range(i, ITERS)] + [(ITERS - 1, ITERS)]


def last_kernel(*refs):
    lats = [refs[8][slot] for slot in range(SPAN)]
    v = next_vector(*refs[:8], lats, *refs[9:12])
    earlier, (out_ref, pair_ref) = refs[12:12 + ITERS - 1], refs[12 + ITERS - 1:]
    out_ref[...] = v
    vectors = [ref[...] for ref in earlier] + [refs[0][...], v]
    lane = lax.broadcasted_iota(jnp.int32, (1, LEV), 1)
    row = jnp.zeros((1, LEV), F32)
    for n, (i, j) in enumerate(PAIRS):
        product = jnp.sum(vectors[i] * vectors[j], axis=0, keepdims=True)
        row = jnp.where(lane == n, jnp.sum(product, axis=1, keepdims=True), row)
    pair_ref[...] = jnp.broadcast_to(row, pair_ref.shape)


def combine_kernel(scale_ref, *refs):
    sums_ref, vector_refs, (x_ref, r_ref, spread) = refs[0], refs[1:ITERS + 2], refs[ITERS + 2:]
    row = jnp.sum(sums_ref[...], axis=0, keepdims=True)
    table = {}
    for n, (i, j) in enumerate(PAIRS):
        table[i, j] = table[j, i] = row[:, n:n + 1]
    for i in range(ITERS - 1):
        table[i, ITERS] = table[i + 1, ITERS - 1]
    scale = scale_ref[0:1, 0:1]
    zero, one = jnp.zeros((1, 1), F32), jnp.ones((1, 1), F32)
    x = [zero] * (ITERS + 1)
    r = [one] + [zero] * ITERS
    d = list(r)

    def form(a, b, na, nb, off):
        total = None
        for i in range(na):
            inner = None
            for j in range(nb):
                term = b[j] * table[i, j + off]
                inner = term if inner is None else inner + term
            term = a[i] * inner
            total = term if total is None else total + term
        return total

    norm = table[0, 0]
    for k in range(ITERS):
        alpha = norm / form(d, d, k + 1, k + 1, 1)
        for i in range(k + 1):
            x[i] = x[i] + alpha * d[i]
            r[i + 1] = r[i + 1] - alpha * d[i]
        if k < ITERS - 1:
            after = form(r, r, k + 2, k + 2, 0)
            ratio = after / norm
            d = [r[i] + ratio * d[i] for i in range(ITERS + 1)]
            norm = after
    x = [scale * value for value in x]
    for c in range(CLON):
        parts = [ref[:, c * LEV:(c + 1) * LEV] for ref in vector_refs]
        total = x[0] * parts[0]
        for i in range(1, ITERS):
            total = total + x[i] * parts[i]
        spread[0, c] = total
        total = r[0] * parts[0]
        for i in range(1, ITERS + 1):
            total = total + r[i] * parts[i]
        spread[1, c] = total
        for s in range(S):
            x_ref[s, c] = spread[0, c, pl.ds(s, CLAT, stride=8), :]
            r_ref[s, c] = spread[1, c, pl.ds(s, CLAT, stride=8), :]


def shape(*dims, dtype=F32):
    return jax.ShapeDtypeStruct(dims, dtype)


def call(kernel, outs, n_in, scalar=False, scratch=(), work=None):
    return pl.pallas_call(
        kernel,
        out_shape=outs,
        in_specs=([sspec()] if scalar else []) + [vspec()] * n_in,
        out_specs=[vspec()] * len(outs),
        scratch_shapes=scratch,
        compiler_params=LIMIT,
        cost_estimate=work,
    )


MATMUL = pl.CostEstimate(flops=2 * 128 * 2 * CELL * SPAN * SLOT, transcendentals=0, bytes_accessed=2 * 2 * CELL * SPAN * SLOT)
BUILD = pl.CostEstimate(flops=16 * TILE * CELL * SPAN * SLOT, transcendentals=0, bytes_accessed=4 * 2 * CELL * SPAN * SLOT)
MESSAGES = (shape(SPAN, 8, SLOT), shape(5, 8, SLOT), shape(5, 8, SLOT), shape(3, 8, SLOT), shape(3, 8, SLOT))
FACE = shape(8, CELL)
FIELD = shape(64, CELL)
SENT = MESSAGES + (FACE, FACE)


def exchange(own, left, right, left2, right2, down, up):
    n_lat = lax.axis_size("lat")
    plus1 = shift(left, "lon", -1)
    minus1 = shift(right, "lon", 1)
    plus2 = shift(left2, "lon", -2)
    minus2 = shift(right2, "lon", 2)
    south = lax.ppermute(up, "lat", [(i, i + 1) for i in range(n_lat - 1)])
    plus1, down = lax.optimization_barrier((plus1, down))
    north = lax.ppermute(down, "lat", [(i + 1, i) for i in range(n_lat - 1)])
    return own, plus1, minus1, plus2, minus2, south, north


def fetching(kernel, outs, scratch, values):
    return pl.pallas_call(
        kernel,
        out_shape=outs,
        in_specs=[pl.BlockSpec(memory_space=pltpu.HBM)] * len(values),
        out_specs=[vspec()] * len(outs),
        scratch_shapes=list(scratch) + [pltpu.SemaphoreType.DMA((len(values),))],
        compiler_params=LIMIT,
    )(*[pltpu.with_memory_space_constraint(value, pltpu.HBM) for value in values])


def body(observed, ray_start, tile_cells, tile_lengths, channel_kernel, noise_weight, prior_weight):
    noise = noise_weight.reshape(1, CHAN)
    kern_space, noise_space = pltpu.VMEM((S, CHAN), F32), pltpu.VMEM((1, CHAN), F32)
    (z,) = fetching(
        source_kernel,
        (shape(8, RAYS),),
        (pltpu.VMEM((CHAN, RAYS), F32), pltpu.VMEM((1, RAYS), jnp.int32), kern_space, noise_space),
        (observed.T, ray_start.reshape(1, RAYS), channel_kernel, noise),
    )
    z1, z3 = shift(z, "lon", -1), shift(z, "lon", 1)
    z0, z4 = shift(z, "lon", -2), shift(z, "lon", 2)
    table, gram, prior, scale = fetching(
        table_kernel,
        (shape(TABLE, RAYS), shape(64, 64), shape(64, LEV), shape(8, LEV)),
        (
            pltpu.SMEM((S,), F32),
            pltpu.VMEM((TILE, SPAN * RAYS), jnp.int32),
            pltpu.VMEM((TILE, SPAN * RAYS), F32),
            kern_space,
            noise_space,
        ),
        (prior_weight, tile_cells.T, tile_lengths.T, channel_kernel, noise),
    )
    shards = lax.all_gather(jnp.concatenate([table, z0, z1, z, z3, z4], axis=0), "orbit")
    w, lat = call(build_kernel, (shape(SPAN, 2 * CELL, SLOT, dtype=BF16), shape(SPAN, 8, SLOT, dtype=jnp.int32)), 1, work=BUILD)(shards)
    v, mask = call(init_kernel, (FIELD, shape(SPAN, 8, SLOT, dtype=jnp.int32)), 3, work=MATMUL)(shards, lat, w)
    vectors = [v]
    sent = call(project_kernel, SENT, 3, work=MATMUL)(v, mask, w)
    for turn in range(ITERS - 1):
        (v,) = call(step_kernel, (FIELD,), 12, work=MATMUL)(v, *exchange(*sent), mask, w, gram, prior)
        vectors.append(v)
        sent = call(project_kernel, SENT, 3, work=MATMUL)(v, mask, w)
    peers = lax.axis_size("lon") * lax.axis_size("lat")
    v, pairs = call(last_kernel, (FIELD, shape(peers, LEV)), 12 + ITERS - 1, work=MATMUL)(
        v, *exchange(*sent), mask, w, gram, prior, *vectors[:-1]
    )
    vectors.append(v)
    pairs = lax.all_to_all(pairs, ("lon", "lat"), 0, 0, tiled=True)
    field = shape(S, CLON, CLAT, LEV)
    return tuple(call(combine_kernel, (field, field), ITERS + 3, False, [pltpu.VMEM((2, CLON, 64, LEV), F32)])(scale, pairs, *vectors))


def solution(mesh):
    return jax.shard_map(
        body,
        mesh=mesh,
        in_specs=(
            P(("orbit", "lon", "lat"), None),
            P(("orbit", "lon", "lat")),
            P(("orbit", "lon", "lat"), None),
            P(("orbit", "lon", "lat"), None),
            P(),
            P(),
            P(),
        ),
        out_specs=(P(None, "lon", "lat", None), P(None, "lon", "lat", None)),
        check_vma=False,
    )
```

```python
import jax
import jax.numpy as jnp
from jax import lax
from jax.experimental import pallas as pl
from jax.experimental.pallas import tpu as pltpu
from jax.sharding import PartitionSpec as P

S = 7
CLON = 4
CLAT = 8
LEV = 128
NT = 3
TILE = 16
ITERS = 4
SPAN = 5
ORB = 8
RAYS = 128
SLOT = ORB * RAYS
CELL = CLON * LEV
CHAN = 64
TABLE = SPAN * 2 * TILE
F32 = jnp.float32
BF16 = jnp.bfloat16
highest = lax.Precision.HIGHEST
VMEM = pltpu.VMEM
LIMIT = pltpu.CompilerParams(vmem_limit_bytes=24 << 20)


def vspec():
    return pl.BlockSpec(memory_space=pltpu.VMEM)


def sspec():
    return pl.BlockSpec(memory_space=pltpu.SMEM)


def shift(block, axis, distance):
    size = lax.axis_size(axis)
    return lax.ppermute(block, axis, [(i, (i + distance) % size) for i in range(size)])


def split(values):
    high = values.astype(BF16)
    low = (values - high.astype(F32)).astype(BF16)
    return high, low


def fetch(sources, places, sem):
    copies = [pltpu.make_async_copy(src, dst, sem.at[n]) for n, (src, dst) in enumerate(zip(sources, places))]
    for copy in copies:
        copy.start()
    for copy in copies:
        copy.wait()


def source_kernel(*refs):
    sources, source_ref, places, sem = refs[:4], refs[4], refs[5:9], refs[9]
    fetch(sources, places, sem)
    obs_ref, start_ref, kern_ref, noise_ref = places
    kern = species_rows(kern_ref)
    source = jnp.dot(kern * noise_ref[...], obs_ref[...], precision=highest, preferred_element_type=F32)
    sub = lax.broadcasted_iota(jnp.int32, (8, RAYS), 0)
    start = jnp.broadcast_to(start_ref[...].astype(F32), (8, RAYS))
    source_ref[...] = jnp.where(sub == S, start, source)


def species_rows(kern_ref):
    sub = lax.broadcasted_iota(jnp.int32, (8, CHAN), 0)
    kern = jnp.zeros((8, CHAN), F32)
    for s in range(S):
        kern = jnp.where(sub == s, kern_ref[s:s + 1, :], kern)
    return kern


def table_kernel(*refs):
    sources, outs, places, sem = refs[:5], refs[5:9], refs[9:14], refs[14]
    fetch(sources, places, sem)
    prior_ref, cells_ref, lengths_ref, kern_ref, noise_ref = places
    table_ref, gram_ref, prior_out, scale_out = outs
    for slot in range(SPAN):
        lanes = slice(slot * RAYS, (slot + 1) * RAYS)
        base = slot * 2 * TILE
        table_ref[base:base + TILE, :] = cells_ref[:, lanes].astype(F32)
        table_ref[base + TILE:base + 2 * TILE, :] = lengths_ref[:, lanes]
    kern = species_rows(kern_ref)
    weighted = kern * noise_ref[...]
    wide = jnp.concatenate([kern] * CLAT, axis=0)
    wide_weighted = jnp.concatenate([weighted] * CLAT, axis=0)
    gram = lax.dot_general(wide_weighted, wide, (((1,), (1,)), ((), ())), precision=highest, preferred_element_type=F32)
    row = lax.broadcasted_iota(jnp.int32, gram.shape, 0)
    col = lax.broadcasted_iota(jnp.int32, gram.shape, 1)
    trace = jnp.sum(jnp.where((row == col) & (row < 8), gram, 0.0))
    top = prior_ref[0]
    for s in range(1, S):
        top = jnp.maximum(top, prior_ref[s])
    bound = jnp.full((8, 128), trace * 128.0 + 12.0 * top, F32)
    scale = 1.0 / bound
    scale_out[...] = scale
    gram_ref[...] = jnp.where((row >> 3) == (col >> 3), gram, 0.0) * scale[0:1, 0:1]
    species = lax.broadcasted_iota(jnp.int32, (CLAT * 8, 128), 0) & 7
    prior = jnp.zeros((CLAT * 8, 128), F32)
    for s in range(S):
        prior = jnp.where(species == s, prior_ref[s], prior)
    prior_out[...] = prior * scale[0:1, 0:1]


def build_kernel(shards, w_ref, lat_ref):
    sub = lax.broadcasted_iota(jnp.int32, (8, RAYS), 0)
    odd = (sub & 1) == 1

    def slot_body(index, carry):
        slot, k = index >> 3, index & 7
        spot = pl.multiple_of(k * RAYS, RAYS)
        base = pl.multiple_of(slot * 2 * TILE, 2 * TILE)
        cells = shards[k, pl.ds(base, TILE), :].astype(jnp.int32)
        lengths = shards[k, pl.ds(base + TILE, TILE), :]
        lat_ref[slot, :, pl.ds(spot, RAYS)] = jnp.broadcast_to((cells[0:1, :] >> 7) & 7, (8, RAYS))
        places = ((cells >> 10) << 7) | (cells & 127)
        first = jnp.broadcast_to(cells[0:1, :] & 1, (8, RAYS)) == 1
        swap = first != odd
        keys = []
        sizes = []
        for j in range(TILE // 2):
            even_key = jnp.broadcast_to(places[2 * j:2 * j + 1, :], (8, RAYS))
            odd_key = jnp.broadcast_to(places[2 * j + 1:2 * j + 2, :], (8, RAYS))
            keys.append(jnp.where(swap, odd_key, even_key) - sub)
            even_len = jnp.broadcast_to(lengths[2 * j:2 * j + 1, :], (8, RAYS))
            odd_len = jnp.broadcast_to(lengths[2 * j + 1:2 * j + 2, :], (8, RAYS))
            sizes.append(jnp.where(swap, odd_len, even_len))
        for i in range(TILE // 2):
            for j in range(i + 1, TILE // 2):
                same = keys[i] == keys[j]
                sizes[i] = sizes[i] + jnp.where(same, sizes[j], 0.0)
                keys[j] = jnp.where(same, -64, keys[j])
        for pair in range(CELL // 16):
            parts = []
            for half in range(2):
                offset = pair * 16 + half * 8
                total = jnp.zeros((8, RAYS), F32)
                for key, size in zip(keys, sizes):
                    total = jnp.where(key == offset, size, total)
                parts.append(total)
            high, low = split(jnp.concatenate(parts, axis=0))
            w_ref[slot, pl.ds(pair * 16, 16), pl.ds(spot, RAYS)] = high
            w_ref[slot, pl.ds(CELL + pair * 16, 16), pl.ds(spot, RAYS)] = low
        return carry

    lax.fori_loop(0, SPAN * ORB, slot_body, 0)


def masked_rows(values, lat):
    rows = jnp.concatenate([jnp.where(lat == l, values, 0.0) for l in range(CLAT)], axis=0)
    return jnp.concatenate(split(rows), axis=0)


def back_all(sums, lats, w_ref):
    total = None
    for slot in range(SPAN):
        part = lax.dot_general(
            w_ref[slot], masked_rows(sums[slot], lats[slot]), (((1,), (1,)), ((), ())), preferred_element_type=F32
        )
        total = part if total is None else total + part
    total = (total[:CELL] + total[CELL:]).T
    return total[:64] + total[64:]


def project_first_kernel(v_ref, mask_ref, w_ref, *outs):
    project_all(v_ref[...], mask_ref, w_ref, *outs)


def project_kernel(part_ref, south, north, prior_ref, mask_ref, w_ref, v_ref, *outs):
    v = with_faces(part_ref[...], south[...], north[...], prior_ref)
    v_ref[...] = v
    project_all(v, mask_ref, w_ref, *outs)


def with_faces(part, south, north, prior_ref):
    weight = jnp.concatenate([prior_ref[0:8, :]] * CLON, axis=1)
    return jnp.concatenate([part[0:8] - weight * south, part[8:56], part[56:64] - weight * north], axis=0)


def project_all(v, mask_ref, w_ref, own_ref, left_ref, right_ref, left2_ref, right2_ref, down_ref, up_ref):
    down_ref[...] = v[0:8]
    up_ref[...] = v[56:64]
    for l in range(CLAT):
        left_ref[4, :, pl.ds(l * LEV, LEV)] = v[8 * l:8 * l + 8, 0:LEV]
        right_ref[4, :, pl.ds(l * LEV, LEV)] = v[8 * l:8 * l + 8, CELL - LEV:]
    halves = jnp.concatenate(split(v), axis=0)
    rows = jnp.concatenate([halves, halves], axis=1)
    for slot in range(SPAN):
        wide = jnp.dot(rows, w_ref[slot], preferred_element_type=F32)
        wide = wide[:64] + wide[64:]
        lat = mask_ref[slot]
        total = jnp.where(lat == 0, wide[0:8], 0.0)
        for l in range(1, CLAT):
            total = total + jnp.where(lat == l, wide[8 * l:8 * l + 8], 0.0)
        own_ref[slot] = total
        if slot >= 1:
            left_ref[slot - 1] = total
        if slot <= 3:
            right_ref[slot] = total
        if slot >= 2:
            left2_ref[slot - 2] = total
        if slot <= 2:
            right2_ref[slot] = total


def init_kernel(shards, lat_ref, w_ref, v_ref, mask_ref):
    sums, lats = [], []
    sub = lax.broadcasted_iota(jnp.int32, (8, SLOT), 0)
    for slot in range(SPAN):
        base = TABLE + 8 * slot
        z = jnp.concatenate([shards[k, base:base + 8, :] for k in range(ORB)], axis=1)
        begin = jnp.broadcast_to(z[S:S + 1, :], (8, SLOT))
        present = (begin <= slot) & (begin + (NT - 1) >= slot)
        lat = jnp.where(present, lat_ref[slot], -1)
        mask_ref[slot] = lat
        lats.append(lat)
        sums.append(jnp.where(sub < S, z, 0.0))
    v_ref[...] = back_all(sums, lats, w_ref)


def ray_sums(own_ref, plus1, minus1, plus2, minus2):
    sums = []
    for slot in range(SPAN):
        total = own_ref[slot]
        if slot <= 3:
            total = total + plus1[slot]
        if slot >= 1:
            total = total + minus1[slot - 1]
        if slot <= 2:
            total = total + plus2[slot]
        if slot >= 2:
            total = total + minus2[slot - 2]
        sums.append(total)
    return sums


def prior_image(v, plus1, minus1, prior_ref):
    west = jnp.concatenate([minus1[4, :, l * LEV:(l + 1) * LEV] for l in range(CLAT)], axis=0)
    east = jnp.concatenate([plus1[4, :, l * LEV:(l + 1) * LEV] for l in range(CLAT)], axis=0)
    cols = [west] + [v[:, c * LEV:(c + 1) * LEV] for c in range(CLON)] + [east]
    lane = lax.broadcasted_iota(jnp.int32, (64, LEV), 1)
    pieces = []
    for c in range(CLON):
        here = cols[c + 1]
        below = jnp.where(lane == 0, 0.0, pltpu.roll(here, 1, 1))
        above = jnp.where(lane == LEV - 1, 0.0, pltpu.roll(here, LEV - 1, 1))
        edge = jnp.zeros((8, LEV), F32)
        south_side = jnp.concatenate([edge, here[:56]], axis=0)
        north_side = jnp.concatenate([here[8:], edge], axis=0)
        near = cols[c] + cols[c + 2] + below + above + south_side + north_side
        pieces.append(prior_ref[...] * (6.0 * here - near))
    return jnp.concatenate(pieces, axis=1)


def step_kernel(v_ref, own_ref, plus1, minus1, plus2, minus2, mask_ref, w_ref, gram_ref, prior_ref, out_ref):
    lats = [mask_ref[slot] for slot in range(SPAN)]
    image = back_all(ray_sums(own_ref, plus1, minus1, plus2, minus2), lats, w_ref)
    image = jnp.dot(gram_ref[...], image, precision=highest, preferred_element_type=F32)
    out_ref[...] = image + prior_image(v_ref[...], plus1, minus1, prior_ref)


PAIRS = [(i, j) for i in range(ITERS) for j in range(i, ITERS)] + [(ITERS - 1, ITERS)]


def last_kernel(part_ref, south, north, prior_ref, *refs):
    earlier, (out_ref, pair_ref) = refs[:ITERS], refs[ITERS:]
    v = with_faces(part_ref[...], south[...], north[...], prior_ref)
    out_ref[...] = v
    vectors = [ref[...] for ref in earlier] + [v]
    lane = lax.broadcasted_iota(jnp.int32, (1, LEV), 1)
    row = jnp.zeros((1, LEV), F32)
    for n, (i, j) in enumerate(PAIRS):
        product = jnp.sum(vectors[i] * vectors[j], axis=0, keepdims=True)
        row = jnp.where(lane == n, jnp.sum(product, axis=1, keepdims=True), row)
    pair_ref[...] = jnp.broadcast_to(row, pair_ref.shape)


def combine_kernel(scale_ref, *refs):
    sums_ref, vector_refs, (x_ref, r_ref, spread) = refs[0], refs[1:ITERS + 2], refs[ITERS + 2:]
    row = jnp.sum(sums_ref[...], axis=0, keepdims=True)
    table = {}
    for n, (i, j) in enumerate(PAIRS):
        table[i, j] = table[j, i] = row[:, n:n + 1]
    for i in range(ITERS - 1):
        table[i, ITERS] = table[i + 1, ITERS - 1]
    scale = scale_ref[0:1, 0:1]
    zero, one = jnp.zeros((1, 1), F32), jnp.ones((1, 1), F32)
    x = [zero] * (ITERS + 1)
    r = [one] + [zero] * ITERS
    d = list(r)

    def form(a, b, na, nb, off):
        total = None
        for i in range(na):
            inner = None
            for j in range(nb):
                term = b[j] * table[i, j + off]
                inner = term if inner is None else inner + term
            term = a[i] * inner
            total = term if total is None else total + term
        return total

    norm = table[0, 0]
    for k in range(ITERS):
        alpha = norm / form(d, d, k + 1, k + 1, 1)
        for i in range(k + 1):
            x[i] = x[i] + alpha * d[i]
            r[i + 1] = r[i + 1] - alpha * d[i]
        if k < ITERS - 1:
            after = form(r, r, k + 2, k + 2, 0)
            ratio = after / norm
            d = [r[i] + ratio * d[i] for i in range(ITERS + 1)]
            norm = after
    x = [scale * value for value in x]
    for c in range(CLON):
        parts = [ref[:, c * LEV:(c + 1) * LEV] for ref in vector_refs]
        total = x[0] * parts[0]
        for i in range(1, ITERS):
            total = total + x[i] * parts[i]
        spread[0, c] = total
        total = r[0] * parts[0]
        for i in range(1, ITERS + 1):
            total = total + r[i] * parts[i]
        spread[1, c] = total
        for s in range(S):
            x_ref[s, c] = spread[0, c, pl.ds(s, CLAT, stride=8), :]
            r_ref[s, c] = spread[1, c, pl.ds(s, CLAT, stride=8), :]


def shape(*dims, dtype=F32):
    return jax.ShapeDtypeStruct(dims, dtype)


def call(kernel, outs, n_in, scalar=False, scratch=(), work=None):
    return pl.pallas_call(
        kernel,
        out_shape=outs,
        in_specs=([sspec()] if scalar else []) + [vspec()] * n_in,
        out_specs=[vspec()] * len(outs),
        scratch_shapes=scratch,
        compiler_params=LIMIT,
        cost_estimate=work,
    )


MATMUL = pl.CostEstimate(flops=2 * 128 * 2 * CELL * SPAN * SLOT, transcendentals=0, bytes_accessed=2 * 2 * CELL * SPAN * SLOT)
BUILD = pl.CostEstimate(flops=16 * TILE * CELL * SPAN * SLOT, transcendentals=0, bytes_accessed=4 * 2 * CELL * SPAN * SLOT)
MESSAGES = (shape(SPAN, 8, SLOT), shape(5, 8, SLOT), shape(5, 8, SLOT), shape(3, 8, SLOT), shape(3, 8, SLOT))
FACE = shape(8, CELL)
FIELD = shape(64, CELL)
SENT = MESSAGES + (FACE, FACE)


def exchange(own, left, right, left2, right2, down, up):
    n_lat = lax.axis_size("lat")
    plus1 = shift(left, "lon", -1)
    minus1 = shift(right, "lon", 1)
    plus2 = shift(left2, "lon", -2)
    minus2 = shift(right2, "lon", 2)
    south = lax.ppermute(up, "lat", [(i, i + 1) for i in range(n_lat - 1)])
    plus1, down = lax.optimization_barrier((plus1, down))
    north = lax.ppermute(down, "lat", [(i + 1, i) for i in range(n_lat - 1)])
    return own, plus1, minus1, plus2, minus2, south, north


def fetching(kernel, outs, scratch, values):
    return pl.pallas_call(
        kernel,
        out_shape=outs,
        in_specs=[pl.BlockSpec(memory_space=pltpu.HBM)] * len(values),
        out_specs=[vspec()] * len(outs),
        scratch_shapes=list(scratch) + [pltpu.SemaphoreType.DMA((len(values),))],
        compiler_params=LIMIT,
    )(*[pltpu.with_memory_space_constraint(value, pltpu.HBM) for value in values])


def body(observed, ray_start, tile_cells, tile_lengths, channel_kernel, noise_weight, prior_weight):
    noise = noise_weight.reshape(1, CHAN)
    kern_space, noise_space = pltpu.VMEM((S, CHAN), F32), pltpu.VMEM((1, CHAN), F32)
    (z,) = fetching(
        source_kernel,
        (shape(8, RAYS),),
        (pltpu.VMEM((CHAN, RAYS), F32), pltpu.VMEM((1, RAYS), jnp.int32), kern_space, noise_space),
        (observed.T, ray_start.reshape(1, RAYS), channel_kernel, noise),
    )
    z1, z3 = shift(z, "lon", -1), shift(z, "lon", 1)
    z0, z4 = shift(z, "lon", -2), shift(z, "lon", 2)
    table, gram, prior, scale = fetching(
        table_kernel,
        (shape(TABLE, RAYS), shape(64, 64), shape(64, LEV), shape(8, LEV)),
        (
            pltpu.SMEM((S,), F32),
            pltpu.VMEM((TILE, SPAN * RAYS), jnp.int32),
            pltpu.VMEM((TILE, SPAN * RAYS), F32),
            kern_space,
            noise_space,
        ),
        (prior_weight, tile_cells.T, tile_lengths.T, channel_kernel, noise),
    )
    shards = lax.all_gather(jnp.concatenate([table, z0, z1, z, z3, z4], axis=0), "orbit")
    w, lat = call(build_kernel, (shape(SPAN, 2 * CELL, SLOT, dtype=BF16), shape(SPAN, 8, SLOT, dtype=jnp.int32)), 1, work=BUILD)(shards)
    v, mask = call(init_kernel, (FIELD, shape(SPAN, 8, SLOT, dtype=jnp.int32)), 3, work=MATMUL)(shards, lat, w)
    vectors = [v]
    sent = call(project_first_kernel, SENT, 3, work=MATMUL)(v, mask, w)
    for turn in range(ITERS):
        *sums, south, north = exchange(*sent)
        (part,) = call(step_kernel, (FIELD,), 10, work=MATMUL)(v, *sums, mask, w, gram, prior)
        if turn < ITERS - 1:
            v, *sent = call(project_kernel, (FIELD,) + SENT, 6, work=MATMUL)(part, south, north, prior, mask, w)
            vectors.append(v)
    peers = lax.axis_size("lon") * lax.axis_size("lat")
    v, pairs = call(last_kernel, (FIELD, shape(peers, LEV)), 4 + ITERS)(part, south, north, prior, *vectors)
    vectors.append(v)
    pairs = lax.all_to_all(pairs, ("lon", "lat"), 0, 0, tiled=True)
    field = shape(S, CLON, CLAT, LEV)
    return tuple(call(combine_kernel, (field, field), ITERS + 3, False, [pltpu.VMEM((2, CLON, 64, LEV), F32)])(scale, pairs, *vectors))


def solution(mesh):
    return jax.shard_map(
        body,
        mesh=mesh,
        in_specs=(
            P(("orbit", "lon", "lat"), None),
            P(("orbit", "lon", "lat")),
            P(("orbit", "lon", "lat"), None),
            P(("orbit", "lon", "lat"), None),
            P(),
            P(),
            P(),
        ),
        out_specs=(P(None, "lon", "lat", None), P(None, "lon", "lat", None)),
        check_vma=False,
    )
```

```python
import jax
import jax.numpy as jnp
from jax import lax
from jax.experimental import pallas as pl
from jax.experimental.pallas import tpu as pltpu
from jax.sharding import PartitionSpec as P

S = 7
CLON = 4
CLAT = 8
LEV = 128
NT = 3
TILE = 16
ITERS = 4
SPAN = 5
ORB = 8
RAYS = 128
SLOT = ORB * RAYS
CELL = CLON * LEV
CHAN = 64
TABLE = SPAN * 2 * TILE
F32 = jnp.float32
BF16 = jnp.bfloat16
highest = lax.Precision.HIGHEST
VMEM = pltpu.VMEM
LIMIT = pltpu.CompilerParams(vmem_limit_bytes=24 << 20)


def vspec():
    return pl.BlockSpec(memory_space=pltpu.VMEM)


def sspec():
    return pl.BlockSpec(memory_space=pltpu.SMEM)


def shift(block, axis, distance):
    size = lax.axis_size(axis)
    return lax.ppermute(block, axis, [(i, (i + distance) % size) for i in range(size)])


def split(values):
    high = values.astype(BF16)
    low = (values - high.astype(F32)).astype(BF16)
    return high, low


def fetch(sources, places, sem):
    copies = [pltpu.make_async_copy(src, dst, sem.at[n]) for n, (src, dst) in enumerate(zip(sources, places))]
    for copy in copies:
        copy.start()
    for copy in copies:
        copy.wait()


def species_rows(kern_ref):
    sub = lax.broadcasted_iota(jnp.int32, (8, CHAN), 0)
    kern = jnp.zeros((8, CHAN), F32)
    for s in range(S):
        kern = jnp.where(sub == s, kern_ref[s:s + 1, :], kern)
    return kern


def table_kernel(*refs):
    sources, outs, places, sem = refs[:7], refs[7:11], refs[11:18], refs[18]
    fetch(sources, places, sem)
    prior_ref, cells_ref, lengths_ref, kern_ref, noise_ref, obs_ref, start_ref = places
    table_ref, gram_ref, prior_out, scale_out = outs
    for slot in range(SPAN):
        lanes = slice(slot * RAYS, (slot + 1) * RAYS)
        base = slot * 2 * TILE
        table_ref[base:base + TILE, :] = cells_ref[:, lanes].astype(F32)
        table_ref[base + TILE:base + 2 * TILE, :] = lengths_ref[:, lanes]
    kern = species_rows(kern_ref)
    weighted = kern * noise_ref[...]
    source = jnp.dot(weighted, obs_ref[...], precision=highest, preferred_element_type=F32)
    sub = lax.broadcasted_iota(jnp.int32, (8, RAYS), 0)
    start = jnp.broadcast_to(start_ref[...].astype(F32), (8, RAYS))
    table_ref[TABLE:TABLE + 8, :] = jnp.where(sub == S, start, source)
    wide = jnp.concatenate([kern] * CLAT, axis=0)
    wide_weighted = jnp.concatenate([weighted] * CLAT, axis=0)
    gram = lax.dot_general(wide_weighted, wide, (((1,), (1,)), ((), ())), precision=highest, preferred_element_type=F32)
    row = lax.broadcasted_iota(jnp.int32, gram.shape, 0)
    col = lax.broadcasted_iota(jnp.int32, gram.shape, 1)
    trace = jnp.sum(jnp.where((row == col) & (row < 8), gram, 0.0))
    top = prior_ref[0]
    for s in range(1, S):
        top = jnp.maximum(top, prior_ref[s])
    bound = jnp.full((8, 128), trace * 128.0 + 12.0 * top, F32)
    scale = 1.0 / bound
    scale_out[...] = scale
    gram_ref[...] = jnp.where((row >> 3) == (col >> 3), gram, 0.0) * scale[0:1, 0:1]
    species = lax.broadcasted_iota(jnp.int32, (CLAT * 8, 128), 0) & 7
    prior = jnp.zeros((CLAT * 8, 128), F32)
    for s in range(S):
        prior = jnp.where(species == s, prior_ref[s], prior)
    prior_out[...] = prior * scale[0:1, 0:1]


def gather_kernel(shards, out):
    for k in range(ORB):
        out[:, k * RAYS:(k + 1) * RAYS] = shards[k, TABLE:TABLE + 8, :]


def build_kernel(shards, w_ref, lat_ref):
    sub = lax.broadcasted_iota(jnp.int32, (16, RAYS), 0)
    odd = (sub[:8] & 1) == 1

    def slot_body(index, carry):
        slot, k = index >> 3, index & 7
        spot = pl.multiple_of(k * RAYS, RAYS)
        base = pl.multiple_of(slot * 2 * TILE, 2 * TILE)
        cells = shards[k, pl.ds(base, TILE), :].astype(jnp.int32)
        lengths = shards[k, pl.ds(base + TILE, TILE), :]
        lat_ref[slot, :, pl.ds(spot, RAYS)] = jnp.broadcast_to((cells[0:1, :] >> 7) & 7, (8, RAYS))
        places = ((cells >> 10) << 7) | (cells & 127)
        first = jnp.broadcast_to(cells[0:1, :] & 1, (8, RAYS)) == 1
        swap = first != odd
        keys = []
        sizes = []
        for j in range(TILE // 2):
            even_key = jnp.broadcast_to(places[2 * j:2 * j + 1, :], (8, RAYS))
            odd_key = jnp.broadcast_to(places[2 * j + 1:2 * j + 2, :], (8, RAYS))
            keys.append(jnp.where(swap, odd_key, even_key))
            even_len = jnp.broadcast_to(lengths[2 * j:2 * j + 1, :], (8, RAYS))
            odd_len = jnp.broadcast_to(lengths[2 * j + 1:2 * j + 2, :], (8, RAYS))
            sizes.append(jnp.where(swap, odd_len, even_len))
        for i in range(TILE // 2):
            for j in range(i + 1, TILE // 2):
                same = keys[i] == keys[j]
                sizes[i] = sizes[i] + jnp.where(same, sizes[j], 0.0)
                keys[j] = jnp.where(same, -1024, keys[j])
        highs, lows = zip(*[split(jnp.concatenate([size, size], axis=0)) for size in sizes])
        keys = [jnp.concatenate([key, key], axis=0) for key in keys]
        zero = jnp.zeros((16, RAYS), BF16)
        for c in range(CLON):
            levels = [jnp.where((key >> 7) == c, (key & 127) - sub, -64).astype(F32).astype(BF16) for key in keys]
            for part in range(LEV // 16):
                high, low = zero, zero
                target = jnp.full((16, RAYS), part * 16, BF16)
                for j in range(TILE // 2):
                    hit = levels[j] == target
                    high = jnp.where(hit, highs[j], high)
                    low = jnp.where(hit, lows[j], low)
                row = c * LEV + part * 16
                w_ref[slot, pl.ds(row, 16), pl.ds(spot, RAYS)] = high
                w_ref[slot, pl.ds(CELL + row, 16), pl.ds(spot, RAYS)] = low
        return carry

    lax.fori_loop(0, SPAN * ORB, slot_body, 0)


def masked_rows(values, lat):
    rows = jnp.concatenate([jnp.where(lat == l, values, 0.0) for l in range(CLAT)], axis=0)
    return jnp.concatenate(split(rows), axis=0)


def back_all(sums, lats, w_ref):
    total = None
    for slot in range(SPAN):
        part = lax.dot_general(
            w_ref[slot], masked_rows(sums[slot], lats[slot]), (((1,), (1,)), ((), ())), preferred_element_type=F32
        )
        total = part if total is None else total + part
    total = (total[:CELL] + total[CELL:]).T
    return total[:64] + total[64:]


def project_first_kernel(side_ref, v_ref, mask_ref, w_ref, *outs):
    project_all(side_ref[0] == 1, v_ref[...], mask_ref, w_ref, *outs)


def project_kernel(side_ref, part_ref, first, second, prior_ref, mask_ref, w_ref, v_ref, *outs):
    odd = side_ref[0] == 1
    v = with_faces(odd, part_ref[...], first[...], second[...], prior_ref)
    v_ref[...] = v
    project_all(odd, v, mask_ref, w_ref, *outs)


def with_faces(odd, part, first, second, prior_ref):
    south, north = jnp.where(odd, first, second), jnp.where(odd, second, first)
    weight = jnp.concatenate([prior_ref[0:8, :]] * CLON, axis=1)
    return jnp.concatenate([part[0:8] - weight * south, part[8:56], part[56:64] - weight * north], axis=0)


def project_all(odd, v, mask_ref, w_ref, own_ref, left_ref, right_ref, left2_ref, right2_ref, first_ref, second_ref):
    first_ref[...] = jnp.where(odd, v[0:8], v[56:64])
    second_ref[...] = jnp.where(odd, v[56:64], v[0:8])
    for l in range(CLAT):
        left_ref[4, :, pl.ds(l * LEV, LEV)] = v[8 * l:8 * l + 8, 0:LEV]
        right_ref[4, :, pl.ds(l * LEV, LEV)] = v[8 * l:8 * l + 8, CELL - LEV:]
    halves = jnp.concatenate(split(v), axis=0)
    rows = jnp.concatenate([halves, halves], axis=1)
    for slot in range(SPAN):
        wide = jnp.dot(rows, w_ref[slot], preferred_element_type=F32)
        wide = wide[:64] + wide[64:]
        lat = mask_ref[slot]
        total = jnp.where(lat == 0, wide[0:8], 0.0)
        for l in range(1, CLAT):
            total = total + jnp.where(lat == l, wide[8 * l:8 * l + 8], 0.0)
        own_ref[slot] = total
        if slot >= 1:
            left_ref[slot - 1] = total
        if slot <= 3:
            right_ref[slot] = total
        if slot >= 2:
            left2_ref[slot - 2] = total
        if slot <= 2:
            right2_ref[slot] = total


def init_kernel(z2, z0, z1, z3, z4, lat_ref, w_ref, v_ref, mask_ref):
    sums, lats = [], []
    sub = lax.broadcasted_iota(jnp.int32, (8, SLOT), 0)
    for slot, z_ref in enumerate((z0, z1, z2, z3, z4)):
        z = z_ref[...]
        begin = jnp.broadcast_to(z[S:S + 1, :], (8, SLOT))
        present = (begin <= slot) & (begin + (NT - 1) >= slot)
        lat = jnp.where(present, lat_ref[slot], -1)
        mask_ref[slot] = lat
        lats.append(lat)
        sums.append(jnp.where(sub < S, z, 0.0))
    v_ref[...] = back_all(sums, lats, w_ref)


def ray_sums(own_ref, plus1, minus1, plus2, minus2):
    sums = []
    for slot in range(SPAN):
        total = own_ref[slot]
        if slot <= 3:
            total = total + plus1[slot]
        if slot >= 1:
            total = total + minus1[slot - 1]
        if slot <= 2:
            total = total + plus2[slot]
        if slot >= 2:
            total = total + minus2[slot - 2]
        sums.append(total)
    return sums


def prior_image(v, plus1, minus1, prior_ref):
    west = jnp.concatenate([minus1[4, :, l * LEV:(l + 1) * LEV] for l in range(CLAT)], axis=0)
    east = jnp.concatenate([plus1[4, :, l * LEV:(l + 1) * LEV] for l in range(CLAT)], axis=0)
    cols = [west] + [v[:, c * LEV:(c + 1) * LEV] for c in range(CLON)] + [east]
    lane = lax.broadcasted_iota(jnp.int32, (64, LEV), 1)
    pieces = []
    for c in range(CLON):
        here = cols[c + 1]
        below = jnp.where(lane == 0, 0.0, pltpu.roll(here, 1, 1))
        above = jnp.where(lane == LEV - 1, 0.0, pltpu.roll(here, LEV - 1, 1))
        edge = jnp.zeros((8, LEV), F32)
        south_side = jnp.concatenate([edge, here[:56]], axis=0)
        north_side = jnp.concatenate([here[8:], edge], axis=0)
        near = cols[c] + cols[c + 2] + below + above + south_side + north_side
        pieces.append(prior_ref[...] * (6.0 * here - near))
    return jnp.concatenate(pieces, axis=1)


def step_kernel(v_ref, own_ref, plus1, minus1, plus2, minus2, mask_ref, w_ref, gram_ref, prior_ref, out_ref):
    lats = [mask_ref[slot] for slot in range(SPAN)]
    image = back_all(ray_sums(own_ref, plus1, minus1, plus2, minus2), lats, w_ref)
    image = jnp.dot(gram_ref[...], image, precision=highest, preferred_element_type=F32)
    out_ref[...] = image + prior_image(v_ref[...], plus1, minus1, prior_ref)


PAIRS = [(i, j) for i in range(ITERS) for j in range(i, ITERS)] + [(ITERS - 1, ITERS)]


def last_kernel(side_ref, part_ref, first, second, prior_ref, *refs):
    earlier, (out_ref, pair_ref) = refs[:ITERS], refs[ITERS:]
    v = with_faces(side_ref[0] == 1, part_ref[...], first[...], second[...], prior_ref)
    out_ref[...] = v
    vectors = [ref[...] for ref in earlier] + [v]
    lane = lax.broadcasted_iota(jnp.int32, (1, LEV), 1)
    row = jnp.zeros((1, LEV), F32)
    for n, (i, j) in enumerate(PAIRS):
        product = jnp.sum(vectors[i] * vectors[j], axis=0, keepdims=True)
        row = jnp.where(lane == n, jnp.sum(product, axis=1, keepdims=True), row)
    pair_ref[...] = jnp.broadcast_to(row, pair_ref.shape)


def combine_kernel(scale_ref, *refs):
    sums_ref, vector_refs, (x_ref, r_ref, spread) = refs[0], refs[1:ITERS + 2], refs[ITERS + 2:]
    row = jnp.sum(sums_ref[...], axis=0, keepdims=True)
    table = {}
    for n, (i, j) in enumerate(PAIRS):
        table[i, j] = table[j, i] = row[:, n:n + 1]
    for i in range(ITERS - 1):
        table[i, ITERS] = table[i + 1, ITERS - 1]
    scale = scale_ref[0:1, 0:1]
    zero, one = jnp.zeros((1, 1), F32), jnp.ones((1, 1), F32)
    x = [zero] * (ITERS + 1)
    r = [one] + [zero] * ITERS
    d = list(r)

    def form(a, b, na, nb, off):
        total = None
        for i in range(na):
            inner = None
            for j in range(nb):
                term = b[j] * table[i, j + off]
                inner = term if inner is None else inner + term
            term = a[i] * inner
            total = term if total is None else total + term
        return total

    norm = table[0, 0]
    for k in range(ITERS):
        alpha = norm / form(d, d, k + 1, k + 1, 1)
        for i in range(k + 1):
            x[i] = x[i] + alpha * d[i]
            r[i + 1] = r[i + 1] - alpha * d[i]
        if k < ITERS - 1:
            after = form(r, r, k + 2, k + 2, 0)
            ratio = after / norm
            d = [r[i] + ratio * d[i] for i in range(ITERS + 1)]
            norm = after
    x = [scale * value for value in x]
    for c in range(CLON):
        parts = [ref[:, c * LEV:(c + 1) * LEV] for ref in vector_refs]
        total = x[0] * parts[0]
        for i in range(1, ITERS):
            total = total + x[i] * parts[i]
        spread[0, c] = total
        total = r[0] * parts[0]
        for i in range(1, ITERS + 1):
            total = total + r[i] * parts[i]
        spread[1, c] = total
        for s in range(S):
            x_ref[s, c] = spread[0, c, pl.ds(s, CLAT, stride=8), :]
            r_ref[s, c] = spread[1, c, pl.ds(s, CLAT, stride=8), :]


def shape(*dims, dtype=F32):
    return jax.ShapeDtypeStruct(dims, dtype)


def call(kernel, outs, n_in, scalar=False, scratch=(), work=None):
    return pl.pallas_call(
        kernel,
        out_shape=outs,
        in_specs=([sspec()] if scalar else []) + [vspec()] * n_in,
        out_specs=[vspec()] * len(outs),
        scratch_shapes=scratch,
        compiler_params=LIMIT,
        cost_estimate=work,
    )


MATMUL = pl.CostEstimate(flops=2 * 128 * 2 * CELL * SPAN * SLOT, transcendentals=0, bytes_accessed=2 * 2 * CELL * SPAN * SLOT)
BUILD = pl.CostEstimate(flops=16 * TILE * CELL * SPAN * SLOT, transcendentals=0, bytes_accessed=4 * 2 * CELL * SPAN * SLOT)
MESSAGES = (shape(SPAN, 8, SLOT), shape(5, 8, SLOT), shape(5, 8, SLOT), shape(3, 8, SLOT), shape(3, 8, SLOT))
FACE = shape(8, CELL)
FIELD = shape(64, CELL)
SENT = MESSAGES + (FACE, FACE)


def pairs_from(start, size):
    route = [(i, i + 1) for i in range(start, size - 1, 2)]
    return route + [(j, i) for i, j in route]


def exchange(own, left, right, left2, right2, first, second):
    n_lat = lax.axis_size("lat")
    plus1 = shift(left, "lon", -1)
    minus1 = shift(right, "lon", 1)
    plus2 = shift(left2, "lon", -2)
    minus2 = shift(right2, "lon", 2)
    first = lax.ppermute(first, "lat", pairs_from(0, n_lat))
    plus1, second = lax.optimization_barrier((plus1, second))
    second = lax.ppermute(second, "lat", pairs_from(1, n_lat))
    return own, plus1, minus1, plus2, minus2, first, second


def fetching(kernel, outs, scratch, values):
    return pl.pallas_call(
        kernel,
        out_shape=outs,
        in_specs=[pl.BlockSpec(memory_space=pltpu.HBM)] * len(values),
        out_specs=[vspec()] * len(outs),
        scratch_shapes=list(scratch) + [pltpu.SemaphoreType.DMA((len(values),))],
        compiler_params=LIMIT,
    )(*[pltpu.with_memory_space_constraint(value, pltpu.HBM) for value in values])


def body(observed, ray_start, tile_cells, tile_lengths, channel_kernel, noise_weight, prior_weight):
    side = (lax.axis_index("lat") & 1).astype(jnp.int32).reshape(1)
    table, gram, prior, scale = fetching(
        table_kernel,
        (shape(TABLE + 8, RAYS), shape(64, 64), shape(64, LEV), shape(8, LEV)),
        (
            pltpu.SMEM((S,), F32),
            pltpu.VMEM((TILE, SPAN * RAYS), jnp.int32),
            pltpu.VMEM((TILE, SPAN * RAYS), F32),
            pltpu.VMEM((S, CHAN), F32),
            pltpu.VMEM((1, CHAN), F32),
            pltpu.VMEM((CHAN, RAYS), F32),
            pltpu.VMEM((1, RAYS), jnp.int32),
        ),
        (prior_weight, tile_cells.T, tile_lengths.T, channel_kernel, noise_weight.reshape(1, CHAN), observed.T, ray_start.reshape(1, RAYS)),
    )
    shards = lax.all_gather(table, "orbit")
    (z,) = call(gather_kernel, (shape(8, SLOT),), 1)(shards)
    z1, z3 = shift(z, "lon", -1), shift(z, "lon", 1)
    z0, z4 = shift(z, "lon", -2), shift(z, "lon", 2)
    w, lat = call(build_kernel, (shape(SPAN, 2 * CELL, SLOT, dtype=BF16), shape(SPAN, 8, SLOT, dtype=jnp.int32)), 1, work=BUILD)(shards)
    v, mask = call(init_kernel, (FIELD, shape(SPAN, 8, SLOT, dtype=jnp.int32)), 7, work=MATMUL)(z, z0, z1, z3, z4, lat, w)
    vectors = [v]
    sent = call(project_first_kernel, SENT, 3, True, work=MATMUL)(side, v, mask, w)
    for turn in range(ITERS):
        *sums, first, second = exchange(*sent)
        (part,) = call(step_kernel, (FIELD,), 10, work=MATMUL)(v, *sums, mask, w, gram, prior)
        if turn < ITERS - 1:
            v, *sent = call(project_kernel, (FIELD,) + SENT, 6, True, work=MATMUL)(side, part, first, second, prior, mask, w)
            vectors.append(v)
    peers = lax.axis_size("lon") * lax.axis_size("lat")
    v, pairs = call(last_kernel, (FIELD, shape(peers, LEV)), 4 + ITERS, True)(side, part, first, second, prior, *vectors)
    vectors.append(v)
    pairs = lax.all_to_all(pairs, ("lon", "lat"), 0, 0, tiled=True)
    field = shape(S, CLON, CLAT, LEV)
    return tuple(call(combine_kernel, (field, field), ITERS + 3, False, [pltpu.VMEM((2, CLON, 64, LEV), F32)])(scale, pairs, *vectors))


def solution(mesh):
    return jax.shard_map(
        body,
        mesh=mesh,
        in_specs=(
            P(("orbit", "lon", "lat"), None),
            P(("orbit", "lon", "lat")),
            P(("orbit", "lon", "lat"), None),
            P(("orbit", "lon", "lat"), None),
            P(),
            P(),
            P(),
        ),
        out_specs=(P(None, "lon", "lat", None), P(None, "lon", "lat", None)),
        check_vma=False,
    )
```

```python
import jax
import jax.numpy as jnp
from jax import lax
from jax.experimental import pallas as pl
from jax.experimental.pallas import tpu as pltpu
from jax.sharding import PartitionSpec as P

S = 7
CLON = 4
CLAT = 8
LEV = 128
NT = 3
TILE = 16
ITERS = 4
SPAN = 5
ORB = 8
RAYS = 128
SLOT = ORB * RAYS
CELL = CLON * LEV
CHAN = 64
TABLE = SPAN * 2 * TILE
F32 = jnp.float32
BF16 = jnp.bfloat16
highest = lax.Precision.HIGHEST
VMEM = pltpu.VMEM
LIMIT = pltpu.CompilerParams(vmem_limit_bytes=16 << 20)


def vspec():
    return pl.BlockSpec(memory_space=pltpu.VMEM)


def sspec():
    return pl.BlockSpec(memory_space=pltpu.SMEM)


def shift(block, axis, distance):
    size = lax.axis_size(axis)
    return lax.ppermute(block, axis, [(i, (i + distance) % size) for i in range(size)])


def split(values):
    high = values.astype(BF16)
    low = (values - high.astype(F32)).astype(BF16)
    return high, low


def fetch(sources, places, sem):
    copies = [pltpu.make_async_copy(src, dst, sem.at[n]) for n, (src, dst) in enumerate(zip(sources, places))]
    for copy in copies:
        copy.start()
    for copy in copies:
        copy.wait()


def species_rows(kern_ref):
    sub = lax.broadcasted_iota(jnp.int32, (8, CHAN), 0)
    kern = jnp.zeros((8, CHAN), F32)
    for s in range(S):
        kern = jnp.where(sub == s, kern_ref[s:s + 1, :], kern)
    return kern


def table_kernel(*refs):
    sources, outs, places, sem = refs[:7], refs[7:11], refs[11:18], refs[18]
    fetch(sources, places, sem)
    prior_ref, cells_ref, lengths_ref, kern_ref, noise_ref, obs_ref, start_ref = places
    table_ref, gram_ref, prior_out, scale_out = outs
    for slot in range(SPAN):
        lanes = slice(slot * RAYS, (slot + 1) * RAYS)
        base = slot * 2 * TILE
        table_ref[base:base + TILE, :] = cells_ref[:, lanes].astype(F32)
        table_ref[base + TILE:base + 2 * TILE, :] = lengths_ref[:, lanes]
    kern = species_rows(kern_ref)
    weighted = kern * noise_ref[...]
    source = jnp.dot(weighted, obs_ref[...], precision=highest, preferred_element_type=F32)
    sub = lax.broadcasted_iota(jnp.int32, (8, RAYS), 0)
    start = jnp.broadcast_to(start_ref[...].astype(F32), (8, RAYS))
    table_ref[TABLE:TABLE + 8, :] = jnp.where(sub == S, start, source)
    wide = jnp.concatenate([kern] * CLAT, axis=0)
    wide_weighted = jnp.concatenate([weighted] * CLAT, axis=0)
    gram = lax.dot_general(wide_weighted, wide, (((1,), (1,)), ((), ())), precision=highest, preferred_element_type=F32)
    row = lax.broadcasted_iota(jnp.int32, gram.shape, 0)
    col = lax.broadcasted_iota(jnp.int32, gram.shape, 1)
    trace = jnp.sum(jnp.where((row == col) & (row < 8), gram, 0.0))
    top = prior_ref[0]
    for s in range(1, S):
        top = jnp.maximum(top, prior_ref[s])
    bound = jnp.full((8, 128), trace * 128.0 + 12.0 * top, F32)
    scale = 1.0 / bound
    scale_out[...] = scale
    gram_ref[...] = jnp.where((row >> 3) == (col >> 3), gram, 0.0) * scale[0:1, 0:1]
    species = lax.broadcasted_iota(jnp.int32, (CLAT * 8, 128), 0) & 7
    prior = jnp.zeros((CLAT * 8, 128), F32)
    for s in range(S):
        prior = jnp.where(species == s, prior_ref[s], prior)
    prior_out[...] = prior * scale[0:1, 0:1]


def gather_kernel(shards, out):
    for k in range(ORB):
        out[:, k * RAYS:(k + 1) * RAYS] = shards[k, TABLE:TABLE + 8, :]


def build_kernel(shards, w_ref, wt_ref, lat_ref):
    sub = lax.broadcasted_iota(jnp.int32, (16, RAYS), 0)
    odd = (sub[:8] & 1) == 1

    def slot_body(index, carry):
        slot, k = index >> 3, index & 7
        spot = pl.multiple_of(k * RAYS, RAYS)
        base = pl.multiple_of(slot * 2 * TILE, 2 * TILE)
        cells = shards[k, pl.ds(base, TILE), :].astype(jnp.int32)
        lengths = shards[k, pl.ds(base + TILE, TILE), :]
        lat_ref[slot, :, pl.ds(spot, RAYS)] = jnp.broadcast_to((cells[0:1, :] >> 7) & 7, (8, RAYS))
        places = ((cells >> 10) << 7) | (cells & 127)
        first = jnp.broadcast_to(cells[0:1, :] & 1, (8, RAYS)) == 1
        swap = first != odd
        keys = []
        sizes = []
        for j in range(TILE // 2):
            even_key = jnp.broadcast_to(places[2 * j:2 * j + 1, :], (8, RAYS))
            odd_key = jnp.broadcast_to(places[2 * j + 1:2 * j + 2, :], (8, RAYS))
            keys.append(jnp.where(swap, odd_key, even_key))
            even_len = jnp.broadcast_to(lengths[2 * j:2 * j + 1, :], (8, RAYS))
            odd_len = jnp.broadcast_to(lengths[2 * j + 1:2 * j + 2, :], (8, RAYS))
            sizes.append(jnp.where(swap, odd_len, even_len))
        for i in range(TILE // 2):
            for j in range(i + 1, TILE // 2):
                same = keys[i] == keys[j]
                sizes[i] = sizes[i] + jnp.where(same, sizes[j], 0.0)
                keys[j] = jnp.where(same, -1024, keys[j])
        highs, lows = zip(*[split(jnp.concatenate([size, size], axis=0)) for size in sizes])
        keys = [jnp.concatenate([key, key], axis=0) for key in keys]
        zero = jnp.zeros((16, RAYS), BF16)
        for c in range(CLON):
            levels = [jnp.where((key >> 7) == c, (key & 127) - sub, -64).astype(F32).astype(BF16) for key in keys]
            high_parts, low_parts = [], []
            for part in range(LEV // 16):
                high, low = zero, zero
                target = jnp.full((16, RAYS), part * 16, BF16)
                for j in range(TILE // 2):
                    hit = levels[j] == target
                    high = jnp.where(hit, highs[j], high)
                    low = jnp.where(hit, lows[j], low)
                row = c * LEV + part * 16
                w_ref[slot, pl.ds(row, 16), pl.ds(spot, RAYS)] = high
                w_ref[slot, pl.ds(CELL + row, 16), pl.ds(spot, RAYS)] = low
                high_parts.append(high)
                low_parts.append(low)
            wt_ref[slot, pl.ds(spot, RAYS), c * LEV:(c + 1) * LEV] = jnp.concatenate(high_parts, axis=0).T
            wt_ref[slot, pl.ds(spot, RAYS), CELL + c * LEV:CELL + (c + 1) * LEV] = jnp.concatenate(low_parts, axis=0).T
        return carry

    lax.fori_loop(0, SPAN * ORB, slot_body, 0)


def masked_rows(values, lat):
    rows = jnp.concatenate([jnp.where(lat == l, values, 0.0) for l in range(CLAT)], axis=0)
    return jnp.concatenate(split(rows), axis=0)


def back_all(sums, lats, wt_ref):
    total = None
    for slot in range(SPAN):
        part = jnp.dot(masked_rows(sums[slot], lats[slot]), wt_ref[slot], preferred_element_type=F32)
        total = part if total is None else total + part
    total = total[:, :CELL] + total[:, CELL:]
    return total[:64] + total[64:]


def project_first_kernel(side_ref, v_ref, mask_ref, w_ref, *outs):
    project_all(side_ref[0] == 1, v_ref[...], mask_ref, w_ref, *outs)


def project_kernel(side_ref, part_ref, first, second, prior_ref, mask_ref, w_ref, v_ref, *outs):
    odd = side_ref[0] == 1
    v = with_faces(odd, part_ref[...], first[...], second[...], prior_ref)
    v_ref[...] = v
    project_all(odd, v, mask_ref, w_ref, *outs)


def with_faces(odd, part, first, second, prior_ref):
    south, north = jnp.where(odd, first, second), jnp.where(odd, second, first)
    weight = jnp.concatenate([prior_ref[0:8, :]] * CLON, axis=1)
    return jnp.concatenate([part[0:8] - weight * south, part[8:56], part[56:64] - weight * north], axis=0)


def project_all(odd, v, mask_ref, w_ref, own_ref, left_ref, right_ref, left2_ref, right2_ref, first_ref, second_ref):
    first_ref[...] = jnp.where(odd, v[0:8], v[56:64])
    second_ref[...] = jnp.where(odd, v[56:64], v[0:8])
    for l in range(CLAT):
        left_ref[4, :, pl.ds(l * LEV, LEV)] = v[8 * l:8 * l + 8, 0:LEV]
        right_ref[4, :, pl.ds(l * LEV, LEV)] = v[8 * l:8 * l + 8, CELL - LEV:]
    halves = jnp.concatenate(split(v), axis=0)
    rows = jnp.concatenate([halves, halves], axis=1)
    for slot in range(SPAN):
        wide = jnp.dot(rows, w_ref[slot], preferred_element_type=F32)
        wide = wide[:64] + wide[64:]
        lat = mask_ref[slot]
        total = jnp.where(lat == 0, wide[0:8], 0.0)
        for l in range(1, CLAT):
            total = total + jnp.where(lat == l, wide[8 * l:8 * l + 8], 0.0)
        own_ref[slot] = total
        if slot >= 1:
            left_ref[slot - 1] = total
        if slot <= 3:
            right_ref[slot] = total
        if slot >= 2:
            left2_ref[slot - 2] = total
        if slot <= 2:
            right2_ref[slot] = total


def init_kernel(z2, z0, z1, z3, z4, lat_ref, w_ref, v_ref, mask_ref):
    sums, lats = [], []
    sub = lax.broadcasted_iota(jnp.int32, (8, SLOT), 0)
    for slot, z_ref in enumerate((z0, z1, z2, z3, z4)):
        z = z_ref[...]
        begin = jnp.broadcast_to(z[S:S + 1, :], (8, SLOT))
        present = (begin <= slot) & (begin + (NT - 1) >= slot)
        lat = jnp.where(present, lat_ref[slot], -1)
        mask_ref[slot] = lat
        lats.append(lat)
        sums.append(jnp.where(sub < S, z, 0.0))
    v_ref[...] = back_all(sums, lats, w_ref)


def ray_sums(own_ref, plus1, minus1, plus2, minus2):
    sums = []
    for slot in range(SPAN):
        total = own_ref[slot]
        if slot <= 3:
            total = total + plus1[slot]
        if slot >= 1:
            total = total + minus1[slot - 1]
        if slot <= 2:
            total = total + plus2[slot]
        if slot >= 2:
            total = total + minus2[slot - 2]
        sums.append(total)
    return sums


def prior_image(v, plus1, minus1, prior_ref):
    west = jnp.concatenate([minus1[4, :, l * LEV:(l + 1) * LEV] for l in range(CLAT)], axis=0)
    east = jnp.concatenate([plus1[4, :, l * LEV:(l + 1) * LEV] for l in range(CLAT)], axis=0)
    cols = [west] + [v[:, c * LEV:(c + 1) * LEV] for c in range(CLON)] + [east]
    lane = lax.broadcasted_iota(jnp.int32, (64, LEV), 1)
    pieces = []
    for c in range(CLON):
        here = cols[c + 1]
        below = jnp.where(lane == 0, 0.0, pltpu.roll(here, 1, 1))
        above = jnp.where(lane == LEV - 1, 0.0, pltpu.roll(here, LEV - 1, 1))
        edge = jnp.zeros((8, LEV), F32)
        south_side = jnp.concatenate([edge, here[:56]], axis=0)
        north_side = jnp.concatenate([here[8:], edge], axis=0)
        near = cols[c] + cols[c + 2] + below + above + south_side + north_side
        pieces.append(prior_ref[...] * (6.0 * here - near))
    return jnp.concatenate(pieces, axis=1)


def step_kernel(v_ref, own_ref, plus1, minus1, plus2, minus2, mask_ref, w_ref, gram_ref, prior_ref, out_ref):
    lats = [mask_ref[slot] for slot in range(SPAN)]
    image = back_all(ray_sums(own_ref, plus1, minus1, plus2, minus2), lats, w_ref)
    image = jnp.dot(gram_ref[...], image, precision=highest, preferred_element_type=F32)
    out_ref[...] = image + prior_image(v_ref[...], plus1, minus1, prior_ref)


PAIRS = [(i, j) for i in range(ITERS) for j in range(i, ITERS)] + [(ITERS - 1, ITERS)]


def last_kernel(side_ref, part_ref, first, second, prior_ref, *refs):
    earlier, (out_ref, pair_ref) = refs[:ITERS], refs[ITERS:]
    v = with_faces(side_ref[0] == 1, part_ref[...], first[...], second[...], prior_ref)
    out_ref[...] = v
    vectors = [ref[...] for ref in earlier] + [v]
    lane = lax.broadcasted_iota(jnp.int32, (1, LEV), 1)
    row = jnp.zeros((1, LEV), F32)
    for n, (i, j) in enumerate(PAIRS):
        product = jnp.sum(vectors[i] * vectors[j], axis=0, keepdims=True)
        row = jnp.where(lane == n, jnp.sum(product, axis=1, keepdims=True), row)
    pair_ref[...] = jnp.broadcast_to(row, pair_ref.shape)


def combine_kernel(scale_ref, *refs):
    sums_ref, vector_refs, (x_ref, r_ref, spread) = refs[0], refs[1:ITERS + 2], refs[ITERS + 2:]
    row = jnp.sum(sums_ref[...], axis=0, keepdims=True)
    table = {}
    for n, (i, j) in enumerate(PAIRS):
        table[i, j] = table[j, i] = row[:, n:n + 1]
    for i in range(ITERS - 1):
        table[i, ITERS] = table[i + 1, ITERS - 1]
    scale = scale_ref[0:1, 0:1]
    zero, one = jnp.zeros((1, 1), F32), jnp.ones((1, 1), F32)
    x = [zero] * (ITERS + 1)
    r = [one] + [zero] * ITERS
    d = list(r)

    def form(a, b, na, nb, off):
        total = None
        for i in range(na):
            inner = None
            for j in range(nb):
                term = b[j] * table[i, j + off]
                inner = term if inner is None else inner + term
            term = a[i] * inner
            total = term if total is None else total + term
        return total

    norm = table[0, 0]
    for k in range(ITERS):
        alpha = norm / form(d, d, k + 1, k + 1, 1)
        for i in range(k + 1):
            x[i] = x[i] + alpha * d[i]
            r[i + 1] = r[i + 1] - alpha * d[i]
        if k < ITERS - 1:
            after = form(r, r, k + 2, k + 2, 0)
            ratio = after / norm
            d = [r[i] + ratio * d[i] for i in range(ITERS + 1)]
            norm = after
    x = [scale * value for value in x]
    for c in range(CLON):
        parts = [ref[:, c * LEV:(c + 1) * LEV] for ref in vector_refs]
        total = x[0] * parts[0]
        for i in range(1, ITERS):
            total = total + x[i] * parts[i]
        spread[0, c] = total
        total = r[0] * parts[0]
        for i in range(1, ITERS + 1):
            total = total + r[i] * parts[i]
        spread[1, c] = total
        for s in range(S):
            x_ref[s, c] = spread[0, c, pl.ds(s, CLAT, stride=8), :]
            r_ref[s, c] = spread[1, c, pl.ds(s, CLAT, stride=8), :]


def shape(*dims, dtype=F32):
    return jax.ShapeDtypeStruct(dims, dtype)


def call(kernel, outs, n_in, scalar=False, scratch=(), work=None):
    return pl.pallas_call(
        kernel,
        out_shape=outs,
        in_specs=([sspec()] if scalar else []) + [vspec()] * n_in,
        out_specs=[vspec()] * len(outs),
        scratch_shapes=scratch,
        compiler_params=LIMIT,
        cost_estimate=work,
    )


MATMUL = pl.CostEstimate(flops=2 * 128 * 2 * CELL * SPAN * SLOT, transcendentals=0, bytes_accessed=2 * 2 * CELL * SPAN * SLOT)
BUILD = pl.CostEstimate(flops=16 * TILE * CELL * SPAN * SLOT, transcendentals=0, bytes_accessed=4 * 2 * CELL * SPAN * SLOT)
MESSAGES = (shape(SPAN, 8, SLOT), shape(5, 8, SLOT), shape(5, 8, SLOT), shape(3, 8, SLOT), shape(3, 8, SLOT))
FACE = shape(8, CELL)
FIELD = shape(64, CELL)
SENT = MESSAGES + (FACE, FACE)


def pairs_from(start, size):
    route = [(i, i + 1) for i in range(start, size - 1, 2)]
    return route + [(j, i) for i, j in route]


def exchange(own, left, right, left2, right2, first, second):
    n_lat = lax.axis_size("lat")
    plus1 = shift(left, "lon", -1)
    minus1 = shift(right, "lon", 1)
    plus2 = shift(left2, "lon", -2)
    minus2 = shift(right2, "lon", 2)
    first = lax.ppermute(first, "lat", pairs_from(0, n_lat))
    plus1, second = lax.optimization_barrier((plus1, second))
    second = lax.ppermute(second, "lat", pairs_from(1, n_lat))
    return own, plus1, minus1, plus2, minus2, first, second


def fetching(kernel, outs, scratch, values):
    return pl.pallas_call(
        kernel,
        out_shape=outs,
        in_specs=[pl.BlockSpec(memory_space=pltpu.HBM)] * len(values),
        out_specs=[vspec()] * len(outs),
        scratch_shapes=list(scratch) + [pltpu.SemaphoreType.DMA((len(values),))],
        compiler_params=LIMIT,
    )(*[pltpu.with_memory_space_constraint(value, pltpu.HBM) for value in values])


def body(observed, ray_start, tile_cells, tile_lengths, channel_kernel, noise_weight, prior_weight):
    side = (lax.axis_index("lat") & 1).astype(jnp.int32).reshape(1)
    table, gram, prior, scale = fetching(
        table_kernel,
        (shape(TABLE + 8, RAYS), shape(64, 64), shape(64, LEV), shape(8, LEV)),
        (
            pltpu.SMEM((S,), F32),
            pltpu.VMEM((TILE, SPAN * RAYS), jnp.int32),
            pltpu.VMEM((TILE, SPAN * RAYS), F32),
            pltpu.VMEM((S, CHAN), F32),
            pltpu.VMEM((1, CHAN), F32),
            pltpu.VMEM((CHAN, RAYS), F32),
            pltpu.VMEM((1, RAYS), jnp.int32),
        ),
        (prior_weight, tile_cells.T, tile_lengths.T, channel_kernel, noise_weight.reshape(1, CHAN), observed.T, ray_start.reshape(1, RAYS)),
    )
    shards = lax.all_gather(table, "orbit")
    (z,) = call(gather_kernel, (shape(8, SLOT),), 1)(shards)
    z1, z3 = shift(z, "lon", -1), shift(z, "lon", 1)
    z0, z4 = shift(z, "lon", -2), shift(z, "lon", 2)
    w, wt, lat = call(build_kernel, (shape(SPAN, 2 * CELL, SLOT, dtype=BF16), shape(SPAN, SLOT, 2 * CELL, dtype=BF16), shape(SPAN, 8, SLOT, dtype=jnp.int32)), 1, work=BUILD)(shards)
    v, mask = call(init_kernel, (FIELD, shape(SPAN, 8, SLOT, dtype=jnp.int32)), 7, work=MATMUL)(z, z0, z1, z3, z4, lat, wt)
    vectors = [v]
    sent = call(project_first_kernel, SENT, 3, True, work=MATMUL)(side, v, mask, w)
    for turn in range(ITERS):
        *sums, first, second = exchange(*sent)
        (part,) = call(step_kernel, (FIELD,), 10, work=MATMUL)(v, *sums, mask, wt, gram, prior)
        if turn < ITERS - 1:
            v, *sent = call(project_kernel, (FIELD,) + SENT, 6, True, work=MATMUL)(side, part, first, second, prior, mask, w)
            vectors.append(v)
    peers = lax.axis_size("lon") * lax.axis_size("lat")
    v, pairs = call(last_kernel, (FIELD, shape(peers, LEV)), 4 + ITERS, True)(side, part, first, second, prior, *vectors)
    vectors.append(v)
    pairs = lax.all_to_all(pairs, ("lon", "lat"), 0, 0, tiled=True)
    field = shape(S, CLON, CLAT, LEV)
    return tuple(call(combine_kernel, (field, field), ITERS + 3, False, [pltpu.VMEM((2, CLON, 64, LEV), F32)])(scale, pairs, *vectors))


def solution(mesh):
    return jax.shard_map(
        body,
        mesh=mesh,
        in_specs=(
            P(("orbit", "lon", "lat"), None),
            P(("orbit", "lon", "lat")),
            P(("orbit", "lon", "lat"), None),
            P(("orbit", "lon", "lat"), None),
            P(),
            P(),
            P(),
        ),
        out_specs=(P(None, "lon", "lat", None), P(None, "lon", "lat", None)),
        check_vma=False,
    )
```

```python
import jax
import jax.numpy as jnp
from jax import lax
from jax.experimental import pallas as pl
from jax.experimental.pallas import tpu as pltpu
from jax.sharding import PartitionSpec as P

S = 7
CLON = 4
CLAT = 8
LEV = 128
NT = 3
TILE = 16
ITERS = 4
SPAN = 5
ORB = 8
RAYS = 128
SLOT = ORB * RAYS
CELL = CLON * LEV
CHAN = 64
TABLE = SPAN * 2 * TILE
F32 = jnp.float32
BF16 = jnp.bfloat16
highest = lax.Precision.HIGHEST
VMEM = pltpu.VMEM
LIMIT = pltpu.CompilerParams(vmem_limit_bytes=16 << 20)


def vspec():
    return pl.BlockSpec(memory_space=pltpu.VMEM)


def sspec():
    return pl.BlockSpec(memory_space=pltpu.SMEM)


def shift(block, axis, distance):
    size = lax.axis_size(axis)
    return lax.ppermute(block, axis, [(i, (i + distance) % size) for i in range(size)])


def split(values):
    high = values.astype(BF16)
    low = (values - high.astype(F32)).astype(BF16)
    return high, low


def fetch(sources, places, sem):
    copies = [pltpu.make_async_copy(src, dst, sem.at[n]) for n, (src, dst) in enumerate(zip(sources, places))]
    for copy in copies:
        copy.start()
    for copy in copies:
        copy.wait()


def species_rows(kern_ref):
    sub = lax.broadcasted_iota(jnp.int32, (8, CHAN), 0)
    kern = jnp.zeros((8, CHAN), F32)
    for s in range(S):
        kern = jnp.where(sub == s, kern_ref[s:s + 1, :], kern)
    return kern


def table_kernel(*refs):
    sources, outs, places, sem = refs[:7], refs[7:11], refs[11:18], refs[18]
    fetch(sources, places, sem)
    prior_ref, cells_ref, lengths_ref, kern_ref, noise_ref, obs_ref, start_ref = places
    table_ref, gram_ref, prior_out, scale_out = outs
    for slot in range(SPAN):
        lanes = slice(slot * RAYS, (slot + 1) * RAYS)
        base = slot * 2 * TILE
        table_ref[base:base + TILE, :] = cells_ref[:, lanes].astype(F32)
        table_ref[base + TILE:base + 2 * TILE, :] = lengths_ref[:, lanes]
    kern = species_rows(kern_ref)
    weighted = kern * noise_ref[...]
    source = jnp.dot(weighted, obs_ref[...], precision=highest, preferred_element_type=F32)
    sub = lax.broadcasted_iota(jnp.int32, (8, RAYS), 0)
    start = jnp.broadcast_to(start_ref[...].astype(F32), (8, RAYS))
    table_ref[TABLE:TABLE + 8, :] = jnp.where(sub == S, start, source)
    wide = jnp.concatenate([kern] * CLAT, axis=0)
    wide_weighted = jnp.concatenate([weighted] * CLAT, axis=0)
    gram = lax.dot_general(wide_weighted, wide, (((1,), (1,)), ((), ())), precision=highest, preferred_element_type=F32)
    row = lax.broadcasted_iota(jnp.int32, gram.shape, 0)
    col = lax.broadcasted_iota(jnp.int32, gram.shape, 1)
    trace = jnp.sum(jnp.where((row == col) & (row < 8), gram, 0.0))
    top = prior_ref[0]
    for s in range(1, S):
        top = jnp.maximum(top, prior_ref[s])
    bound = jnp.full((8, 128), trace * 128.0 + 12.0 * top, F32)
    scale = 1.0 / bound
    scale_out[...] = scale
    gram_ref[...] = jnp.where((row >> 3) == (col >> 3), gram, 0.0) * scale[0:1, 0:1]
    species = lax.broadcasted_iota(jnp.int32, (CLAT * 8, 128), 0) & 7
    prior = jnp.zeros((CLAT * 8, 128), F32)
    for s in range(S):
        prior = jnp.where(species == s, prior_ref[s], prior)
    prior_out[...] = prior * scale[0:1, 0:1]


def gather_kernel(shards, out):
    for k in range(ORB):
        out[:, k * RAYS:(k + 1) * RAYS] = shards[k, TABLE:TABLE + 8, :]


def build_kernel(shards, w_ref, wt_ref, lat_ref):
    sub = lax.broadcasted_iota(jnp.int32, (16, RAYS), 0)
    odd = (sub[:8] & 1) == 1

    def slot_body(index, carry):
        slot, k = index >> 3, index & 7
        spot = pl.multiple_of(k * RAYS, RAYS)
        base = pl.multiple_of(slot * 2 * TILE, 2 * TILE)
        cells = shards[k, pl.ds(base, TILE), :].astype(jnp.int32)
        lengths = shards[k, pl.ds(base + TILE, TILE), :]
        lat_ref[slot, :, pl.ds(spot, RAYS)] = jnp.broadcast_to((cells[0:1, :] >> 7) & 7, (8, RAYS))
        places = ((cells >> 10) << 7) | (cells & 127)
        first = jnp.broadcast_to(cells[0:1, :] & 1, (8, RAYS)) == 1
        swap = first != odd
        keys = []
        sizes = []
        for j in range(TILE // 2):
            even_key = jnp.broadcast_to(places[2 * j:2 * j + 1, :], (8, RAYS))
            odd_key = jnp.broadcast_to(places[2 * j + 1:2 * j + 2, :], (8, RAYS))
            keys.append(jnp.where(swap, odd_key, even_key))
            even_len = jnp.broadcast_to(lengths[2 * j:2 * j + 1, :], (8, RAYS))
            odd_len = jnp.broadcast_to(lengths[2 * j + 1:2 * j + 2, :], (8, RAYS))
            sizes.append(jnp.where(swap, odd_len, even_len))
        for i in range(TILE // 2):
            for j in range(i + 1, TILE // 2):
                same = keys[i] == keys[j]
                sizes[i] = sizes[i] + jnp.where(same, sizes[j], 0.0)
                keys[j] = jnp.where(same, -1024, keys[j])
        highs, lows = zip(*[split(jnp.concatenate([size, size], axis=0)) for size in sizes])
        keys = [jnp.concatenate([key, key], axis=0) for key in keys]
        zero = jnp.zeros((16, RAYS), BF16)
        for c in range(CLON):
            levels = [jnp.where((key >> 7) == c, (key & 127) - sub, -64).astype(F32).astype(BF16) for key in keys]
            high_parts, low_parts = [], []
            for part in range(LEV // 16):
                high, low = zero, zero
                target = jnp.full((16, RAYS), part * 16, BF16)
                for j in range(TILE // 2):
                    hit = levels[j] == target
                    high = jnp.where(hit, highs[j], high)
                    low = jnp.where(hit, lows[j], low)
                row = c * LEV + part * 16
                w_ref[slot, pl.ds(row, 16), pl.ds(spot, RAYS)] = high
                w_ref[slot, pl.ds(CELL + row, 16), pl.ds(spot, RAYS)] = low
                high_parts.append(high)
                low_parts.append(low)
            wt_ref[slot, pl.ds(spot, RAYS), c * LEV:(c + 1) * LEV] = jnp.concatenate(high_parts, axis=0).T
            wt_ref[slot, pl.ds(spot, RAYS), CELL + c * LEV:CELL + (c + 1) * LEV] = jnp.concatenate(low_parts, axis=0).T
        return carry

    lax.fori_loop(0, SPAN * ORB, slot_body, 0, unroll=2)


def masked_rows(values, lat):
    rows = jnp.concatenate([jnp.where(lat == l, values, 0.0) for l in range(CLAT)], axis=0)
    return jnp.concatenate(split(rows), axis=0)


def back_all(sums, lats, wt_ref):
    total = None
    for slot in range(SPAN):
        part = jnp.dot(masked_rows(sums[slot], lats[slot]), wt_ref[slot], preferred_element_type=F32)
        total = part if total is None else total + part
    total = total[:, :CELL] + total[:, CELL:]
    return total[:64] + total[64:]


def project_first_kernel(side_ref, v_ref, mask_ref, w_ref, *outs):
    project_all(side_ref[0] == 1, v_ref[...], mask_ref, w_ref, *outs)


def project_kernel(side_ref, part_ref, first, second, prior_ref, mask_ref, w_ref, v_ref, *outs):
    odd = side_ref[0] == 1
    v = with_faces(odd, part_ref[...], first[...], second[...], prior_ref)
    v_ref[...] = v
    project_all(odd, v, mask_ref, w_ref, *outs)


def with_faces(odd, part, first, second, prior_ref):
    south, north = jnp.where(odd, first, second), jnp.where(odd, second, first)
    weight = jnp.concatenate([prior_ref[0:8, :]] * CLON, axis=1)
    return jnp.concatenate([part[0:8] - weight * south, part[8:56], part[56:64] - weight * north], axis=0)


def project_all(odd, v, mask_ref, w_ref, own_ref, left_ref, right_ref, left2_ref, right2_ref, first_ref, second_ref):
    first_ref[...] = jnp.where(odd, v[0:8], v[56:64])
    second_ref[...] = jnp.where(odd, v[56:64], v[0:8])
    for l in range(CLAT):
        left_ref[4, :, pl.ds(l * LEV, LEV)] = v[8 * l:8 * l + 8, 0:LEV]
        right_ref[4, :, pl.ds(l * LEV, LEV)] = v[8 * l:8 * l + 8, CELL - LEV:]
    halves = jnp.concatenate(split(v), axis=0)
    rows = jnp.concatenate([halves, halves], axis=1)
    for slot in range(SPAN):
        wide = jnp.dot(rows, w_ref[slot], preferred_element_type=F32)
        wide = wide[:64] + wide[64:]
        lat = mask_ref[slot]
        total = jnp.where(lat == 0, wide[0:8], 0.0)
        for l in range(1, CLAT):
            total = total + jnp.where(lat == l, wide[8 * l:8 * l + 8], 0.0)
        own_ref[slot] = total
        if slot >= 1:
            left_ref[slot - 1] = total
        if slot <= 3:
            right_ref[slot] = total
        if slot >= 2:
            left2_ref[slot - 2] = total
        if slot <= 2:
            right2_ref[slot] = total


def init_kernel(z2, z0, z1, z3, z4, lat_ref, w_ref, v_ref, mask_ref):
    sums, lats = [], []
    sub = lax.broadcasted_iota(jnp.int32, (8, SLOT), 0)
    for slot, z_ref in enumerate((z0, z1, z2, z3, z4)):
        z = z_ref[...]
        begin = jnp.broadcast_to(z[S:S + 1, :], (8, SLOT))
        present = (begin <= slot) & (begin + (NT - 1) >= slot)
        lat = jnp.where(present, lat_ref[slot], -1)
        mask_ref[slot] = lat
        lats.append(lat)
        sums.append(jnp.where(sub < S, z, 0.0))
    v_ref[...] = back_all(sums, lats, w_ref)


def ray_sums(own_ref, plus1, minus1, plus2, minus2):
    sums = []
    for slot in range(SPAN):
        total = own_ref[slot]
        if slot <= 3:
            total = total + plus1[slot]
        if slot >= 1:
            total = total + minus1[slot - 1]
        if slot <= 2:
            total = total + plus2[slot]
        if slot >= 2:
            total = total + minus2[slot - 2]
        sums.append(total)
    return sums


def prior_image(v, plus1, minus1, prior_ref):
    west = jnp.concatenate([minus1[4, :, l * LEV:(l + 1) * LEV] for l in range(CLAT)], axis=0)
    east = jnp.concatenate([plus1[4, :, l * LEV:(l + 1) * LEV] for l in range(CLAT)], axis=0)
    cols = [west] + [v[:, c * LEV:(c + 1) * LEV] for c in range(CLON)] + [east]
    lane = lax.broadcasted_iota(jnp.int32, (64, LEV), 1)
    pieces = []
    for c in range(CLON):
        here = cols[c + 1]
        below = jnp.where(lane == 0, 0.0, pltpu.roll(here, 1, 1))
        above = jnp.where(lane == LEV - 1, 0.0, pltpu.roll(here, LEV - 1, 1))
        edge = jnp.zeros((8, LEV), F32)
        south_side = jnp.concatenate([edge, here[:56]], axis=0)
        north_side = jnp.concatenate([here[8:], edge], axis=0)
        near = cols[c] + cols[c + 2] + below + above + south_side + north_side
        pieces.append(prior_ref[...] * (6.0 * here - near))
    return jnp.concatenate(pieces, axis=1)


def step_kernel(v_ref, own_ref, plus1, minus1, plus2, minus2, mask_ref, w_ref, gram_ref, prior_ref, out_ref):
    lats = [mask_ref[slot] for slot in range(SPAN)]
    image = back_all(ray_sums(own_ref, plus1, minus1, plus2, minus2), lats, w_ref)
    image = jnp.dot(gram_ref[...], image, precision=highest, preferred_element_type=F32)
    out_ref[...] = image + prior_image(v_ref[...], plus1, minus1, prior_ref)


PAIRS = [(i, j) for i in range(ITERS) for j in range(i, ITERS)] + [(ITERS - 1, ITERS)]


def last_kernel(side_ref, part_ref, first, second, prior_ref, *refs):
    earlier, (out_ref, pair_ref) = refs[:ITERS], refs[ITERS:]
    v = with_faces(side_ref[0] == 1, part_ref[...], first[...], second[...], prior_ref)
    out_ref[...] = v
    vectors = [ref[...] for ref in earlier] + [v]
    lane = lax.broadcasted_iota(jnp.int32, (1, LEV), 1)
    row = jnp.zeros((1, LEV), F32)
    for n, (i, j) in enumerate(PAIRS):
        product = jnp.sum(vectors[i] * vectors[j], axis=0, keepdims=True)
        row = jnp.where(lane == n, jnp.sum(product, axis=1, keepdims=True), row)
    pair_ref[...] = jnp.broadcast_to(row, pair_ref.shape)


def combine_kernel(scale_ref, *refs):
    sums_ref, vector_refs, (x_ref, r_ref, spread) = refs[0], refs[1:ITERS + 2], refs[ITERS + 2:]
    row = jnp.sum(sums_ref[...], axis=0, keepdims=True)
    table = {}
    for n, (i, j) in enumerate(PAIRS):
        table[i, j] = table[j, i] = row[:, n:n + 1]
    for i in range(ITERS - 1):
        table[i, ITERS] = table[i + 1, ITERS - 1]
    scale = scale_ref[0:1, 0:1]
    zero, one = jnp.zeros((1, 1), F32), jnp.ones((1, 1), F32)
    x = [zero] * (ITERS + 1)
    r = [one] + [zero] * ITERS
    d = list(r)

    def form(a, b, na, nb, off):
        total = None
        for i in range(na):
            inner = None
            for j in range(nb):
                term = b[j] * table[i, j + off]
                inner = term if inner is None else inner + term
            term = a[i] * inner
            total = term if total is None else total + term
        return total

    norm = table[0, 0]
    for k in range(ITERS):
        alpha = norm / form(d, d, k + 1, k + 1, 1)
        for i in range(k + 1):
            x[i] = x[i] + alpha * d[i]
            r[i + 1] = r[i + 1] - alpha * d[i]
        if k < ITERS - 1:
            after = form(r, r, k + 2, k + 2, 0)
            ratio = after / norm
            d = [r[i] + ratio * d[i] for i in range(ITERS + 1)]
            norm = after
    x = [scale * value for value in x]
    for c in range(CLON):
        parts = [ref[:, c * LEV:(c + 1) * LEV] for ref in vector_refs]
        total = x[0] * parts[0]
        for i in range(1, ITERS):
            total = total + x[i] * parts[i]
        spread[0, c] = total
        total = r[0] * parts[0]
        for i in range(1, ITERS + 1):
            total = total + r[i] * parts[i]
        spread[1, c] = total
        for s in range(S):
            x_ref[s, c] = spread[0, c, pl.ds(s, CLAT, stride=8), :]
            r_ref[s, c] = spread[1, c, pl.ds(s, CLAT, stride=8), :]


def shape(*dims, dtype=F32):
    return jax.ShapeDtypeStruct(dims, dtype)


def call(kernel, outs, n_in, scalar=False, scratch=(), work=None):
    return pl.pallas_call(
        kernel,
        out_shape=outs,
        in_specs=([sspec()] if scalar else []) + [vspec()] * n_in,
        out_specs=[vspec()] * len(outs),
        scratch_shapes=scratch,
        compiler_params=LIMIT,
        cost_estimate=work,
    )


MATMUL = pl.CostEstimate(flops=2 * 128 * 2 * CELL * SPAN * SLOT, transcendentals=0, bytes_accessed=2 * 2 * CELL * SPAN * SLOT)
BUILD = pl.CostEstimate(flops=16 * TILE * CELL * SPAN * SLOT, transcendentals=0, bytes_accessed=4 * 2 * CELL * SPAN * SLOT)
MESSAGES = (shape(SPAN, 8, SLOT), shape(5, 8, SLOT), shape(5, 8, SLOT), shape(3, 8, SLOT), shape(3, 8, SLOT))
FACE = shape(8, CELL)
FIELD = shape(64, CELL)
SENT = MESSAGES + (FACE, FACE)


def pairs_from(start, size):
    route = [(i, i + 1) for i in range(start, size - 1, 2)]
    return route + [(j, i) for i, j in route]


def exchange(own, left, right, left2, right2, first, second):
    n_lat = lax.axis_size("lat")
    plus1 = shift(left, "lon", -1)
    minus1 = shift(right, "lon", 1)
    plus2 = shift(left2, "lon", -2)
    minus2 = shift(right2, "lon", 2)
    first = lax.ppermute(first, "lat", pairs_from(0, n_lat))
    plus1, second = lax.optimization_barrier((plus1, second))
    second = lax.ppermute(second, "lat", pairs_from(1, n_lat))
    return own, plus1, minus1, plus2, minus2, first, second


def fetching(kernel, outs, scratch, values):
    return pl.pallas_call(
        kernel,
        out_shape=outs,
        in_specs=[pl.BlockSpec(memory_space=pltpu.HBM)] * len(values),
        out_specs=[vspec()] * len(outs),
        scratch_shapes=list(scratch) + [pltpu.SemaphoreType.DMA((len(values),))],
        compiler_params=LIMIT,
    )(*[pltpu.with_memory_space_constraint(value, pltpu.HBM) for value in values])


def body(observed, ray_start, tile_cells, tile_lengths, channel_kernel, noise_weight, prior_weight):
    side = (lax.axis_index("lat") & 1).astype(jnp.int32).reshape(1)
    table, gram, prior, scale = fetching(
        table_kernel,
        (shape(TABLE + 8, RAYS), shape(64, 64), shape(64, LEV), shape(8, LEV)),
        (
            pltpu.SMEM((S,), F32),
            pltpu.VMEM((TILE, SPAN * RAYS), jnp.int32),
            pltpu.VMEM((TILE, SPAN * RAYS), F32),
            pltpu.VMEM((S, CHAN), F32),
            pltpu.VMEM((1, CHAN), F32),
            pltpu.VMEM((CHAN, RAYS), F32),
            pltpu.VMEM((1, RAYS), jnp.int32),
        ),
        (prior_weight, tile_cells.T, tile_lengths.T, channel_kernel, noise_weight.reshape(1, CHAN), observed.T, ray_start.reshape(1, RAYS)),
    )
    shards = lax.all_gather(table, "orbit")
    (z,) = call(gather_kernel, (shape(8, SLOT),), 1)(shards)
    z1, z3 = shift(z, "lon", -1), shift(z, "lon", 1)
    z0, z4 = shift(z, "lon", -2), shift(z, "lon", 2)
    w, wt, lat = call(build_kernel, (shape(SPAN, 2 * CELL, SLOT, dtype=BF16), shape(SPAN, SLOT, 2 * CELL, dtype=BF16), shape(SPAN, 8, SLOT, dtype=jnp.int32)), 1, work=BUILD)(shards)
    v, mask = call(init_kernel, (FIELD, shape(SPAN, 8, SLOT, dtype=jnp.int32)), 7, work=MATMUL)(z, z0, z1, z3, z4, lat, wt)
    vectors = [v]
    sent = call(project_first_kernel, SENT, 3, True, work=MATMUL)(side, v, mask, w)
    for turn in range(ITERS):
        *sums, first, second = exchange(*sent)
        (part,) = call(step_kernel, (FIELD,), 10, work=MATMUL)(v, *sums, mask, wt, gram, prior)
        if turn < ITERS - 1:
            v, *sent = call(project_kernel, (FIELD,) + SENT, 6, True, work=MATMUL)(side, part, first, second, prior, mask, w)
            vectors.append(v)
    peers = lax.axis_size("lon") * lax.axis_size("lat")
    v, pairs = call(last_kernel, (FIELD, shape(peers, LEV)), 4 + ITERS, True)(side, part, first, second, prior, *vectors)
    vectors.append(v)
    pairs = lax.all_to_all(pairs, ("lon", "lat"), 0, 0, tiled=True)
    field = shape(S, CLON, CLAT, LEV)
    return tuple(call(combine_kernel, (field, field), ITERS + 3, False, [pltpu.VMEM((2, CLON, 64, LEV), F32)])(scale, pairs, *vectors))


def solution(mesh):
    return jax.shard_map(
        body,
        mesh=mesh,
        in_specs=(
            P(("orbit", "lon", "lat"), None),
            P(("orbit", "lon", "lat")),
            P(("orbit", "lon", "lat"), None),
            P(("orbit", "lon", "lat"), None),
            P(),
            P(),
            P(),
        ),
        out_specs=(P(None, "lon", "lat", None), P(None, "lon", "lat", None)),
        check_vma=False,
    )
```

```python
import jax
import jax.numpy as jnp
from jax import lax
from jax.experimental import pallas as pl
from jax.experimental.pallas import tpu as pltpu
from jax.sharding import PartitionSpec as P

S = 7
CLON = 4
CLAT = 8
LEV = 128
NT = 3
TILE = 16
ITERS = 4
SPAN = 5
ORB = 8
RAYS = 128
SLOT = ORB * RAYS
CELL = CLON * LEV
CHAN = 64
TABLE = SPAN * 2 * TILE
F32 = jnp.float32
BF16 = jnp.bfloat16
highest = lax.Precision.HIGHEST
VMEM = pltpu.VMEM
LIMIT = pltpu.CompilerParams(vmem_limit_bytes=16 << 20)


def vspec():
    return pl.BlockSpec(memory_space=pltpu.VMEM)


def sspec():
    return pl.BlockSpec(memory_space=pltpu.SMEM)


def shift(block, axis, distance):
    size = lax.axis_size(axis)
    return lax.ppermute(block, axis, [(i, (i + distance) % size) for i in range(size)])


def split(values):
    high = values.astype(BF16)
    low = (values - high.astype(F32)).astype(BF16)
    return high, low


def fetch(sources, places, sem):
    copies = [pltpu.make_async_copy(src, dst, sem.at[n]) for n, (src, dst) in enumerate(zip(sources, places))]
    for copy in copies:
        copy.start()
    for copy in copies:
        copy.wait()


def species_rows(kern_ref):
    sub = lax.broadcasted_iota(jnp.int32, (8, CHAN), 0)
    kern = jnp.zeros((8, CHAN), F32)
    for s in range(S):
        kern = jnp.where(sub == s, kern_ref[s:s + 1, :], kern)
    return kern


def table_kernel(*refs):
    sources, outs, places, sem = refs[:7], refs[7:11], refs[11:18], refs[18]
    fetch(sources, places, sem)
    prior_ref, cells_ref, lengths_ref, kern_ref, noise_ref, obs_ref, start_ref = places
    table_ref, gram_ref, prior_out, scale_out = outs
    for slot in range(SPAN):
        lanes = slice(slot * RAYS, (slot + 1) * RAYS)
        base = slot * 2 * TILE
        table_ref[base:base + TILE, :] = cells_ref[:, lanes].astype(F32)
        table_ref[base + TILE:base + 2 * TILE, :] = lengths_ref[:, lanes]
    kern = species_rows(kern_ref)
    weighted = kern * noise_ref[...]
    source = jnp.dot(weighted, obs_ref[...], precision=highest, preferred_element_type=F32)
    sub = lax.broadcasted_iota(jnp.int32, (8, RAYS), 0)
    start = jnp.broadcast_to(start_ref[...].astype(F32), (8, RAYS))
    table_ref[TABLE:TABLE + 8, :] = jnp.where(sub == S, start, source)
    wide = jnp.concatenate([kern] * CLAT, axis=0)
    wide_weighted = jnp.concatenate([weighted] * CLAT, axis=0)
    gram = lax.dot_general(wide_weighted, wide, (((1,), (1,)), ((), ())), precision=highest, preferred_element_type=F32)
    row = lax.broadcasted_iota(jnp.int32, gram.shape, 0)
    col = lax.broadcasted_iota(jnp.int32, gram.shape, 1)
    trace = jnp.sum(jnp.where((row == col) & (row < 8), gram, 0.0))
    top = prior_ref[0]
    for s in range(1, S):
        top = jnp.maximum(top, prior_ref[s])
    bound = jnp.full((8, 128), trace * 128.0 + 12.0 * top, F32)
    scale = 1.0 / bound
    scale_out[...] = scale
    gram_ref[...] = jnp.where((row >> 3) == (col >> 3), gram, 0.0) * scale[0:1, 0:1]
    species = lax.broadcasted_iota(jnp.int32, (CLAT * 8, 128), 0) & 7
    prior = jnp.zeros((CLAT * 8, 128), F32)
    for s in range(S):
        prior = jnp.where(species == s, prior_ref[s], prior)
    prior_out[...] = prior * scale[0:1, 0:1]


def gather_kernel(shards, out):
    for k in range(ORB):
        out[:, k * RAYS:(k + 1) * RAYS] = shards[k, TABLE:TABLE + 8, :]


def build_kernel(shards, w_ref, wt_ref, lat_ref):
    sub = lax.broadcasted_iota(jnp.int32, (16, RAYS), 0)
    odd = (sub[:8] & 1) == 1

    def slot_body(index, carry):
        slot, k = index >> 3, index & 7
        spot = pl.multiple_of(k * RAYS, RAYS)
        base = pl.multiple_of(slot * 2 * TILE, 2 * TILE)
        cells = shards[k, pl.ds(base, TILE), :].astype(jnp.int32)
        lengths = shards[k, pl.ds(base + TILE, TILE), :]
        lat_ref[slot, :, pl.ds(spot, RAYS)] = jnp.broadcast_to((cells[0:1, :] >> 7) & 7, (8, RAYS))
        places = ((cells >> 10) << 7) | (cells & 127)
        first = jnp.broadcast_to(cells[0:1, :] & 1, (8, RAYS)) == 1
        swap = first != odd
        keys = []
        sizes = []
        for j in range(TILE // 2):
            even_key = jnp.broadcast_to(places[2 * j:2 * j + 1, :], (8, RAYS))
            odd_key = jnp.broadcast_to(places[2 * j + 1:2 * j + 2, :], (8, RAYS))
            keys.append(jnp.where(swap, odd_key, even_key))
            even_len = jnp.broadcast_to(lengths[2 * j:2 * j + 1, :], (8, RAYS))
            odd_len = jnp.broadcast_to(lengths[2 * j + 1:2 * j + 2, :], (8, RAYS))
            sizes.append(jnp.where(swap, odd_len, even_len))
        for i in range(TILE // 2):
            for j in range(i + 1, TILE // 2):
                same = keys[i] == keys[j]
                sizes[i] = sizes[i] + jnp.where(same, sizes[j], 0.0)
                keys[j] = jnp.where(same, -1024, keys[j])
        highs, lows = zip(*[split(jnp.concatenate([size, size], axis=0)) for size in sizes])
        keys = [jnp.concatenate([key, key], axis=0) for key in keys]
        zero = jnp.zeros((16, RAYS), BF16)
        for c in range(CLON):
            levels = [jnp.where((key >> 7) == c, (key & 127) - sub, -64).astype(F32).astype(BF16) for key in keys]
            high_parts, low_parts = [], []
            for part in range(LEV // 16):
                high, low = zero, zero
                target = jnp.full((16, RAYS), part * 16, BF16)
                for j in range(TILE // 2):
                    hit = levels[j] == target
                    high = jnp.where(hit, highs[j], high)
                    low = jnp.where(hit, lows[j], low)
                row = c * LEV + part * 16
                w_ref[slot, pl.ds(row, 16), pl.ds(spot, RAYS)] = high
                w_ref[slot, pl.ds(CELL + row, 16), pl.ds(spot, RAYS)] = low
                high_parts.append(high)
                low_parts.append(low)
            wt_ref[slot, pl.ds(spot, RAYS), c * LEV:(c + 1) * LEV] = jnp.concatenate(high_parts, axis=0).T
            wt_ref[slot, pl.ds(spot, RAYS), CELL + c * LEV:CELL + (c + 1) * LEV] = jnp.concatenate(low_parts, axis=0).T
        return carry

    lax.fori_loop(0, SPAN * ORB, slot_body, 0, unroll=4)


def masked_rows(values, lat):
    rows = jnp.concatenate([jnp.where(lat == l, values, 0.0) for l in range(CLAT)], axis=0)
    return jnp.concatenate(split(rows), axis=0)


def back_all(sums, lats, wt_ref):
    total = None
    for slot in range(SPAN):
        part = jnp.dot(masked_rows(sums[slot], lats[slot]), wt_ref[slot], preferred_element_type=F32)
        total = part if total is None else total + part
    total = total[:, :CELL] + total[:, CELL:]
    return total[:64] + total[64:]


def project_first_kernel(side_ref, v_ref, mask_ref, w_ref, *outs):
    project_all(side_ref[0] == 1, v_ref[...], mask_ref, w_ref, *outs)


def project_kernel(side_ref, part_ref, first, second, prior_ref, mask_ref, w_ref, v_ref, *outs):
    odd = side_ref[0] == 1
    v = with_faces(odd, part_ref[...], first[...], second[...], prior_ref)
    v_ref[...] = v
    project_all(odd, v, mask_ref, w_ref, *outs)


def with_faces(odd, part, first, second, prior_ref):
    south, north = jnp.where(odd, first, second), jnp.where(odd, second, first)
    weight = jnp.concatenate([prior_ref[0:8, :]] * CLON, axis=1)
    return jnp.concatenate([part[0:8] - weight * south, part[8:56], part[56:64] - weight * north], axis=0)


def project_all(odd, v, mask_ref, w_ref, own_ref, left_ref, right_ref, left2_ref, right2_ref, first_ref, second_ref):
    first_ref[...] = jnp.where(odd, v[0:8], v[56:64])
    second_ref[...] = jnp.where(odd, v[56:64], v[0:8])
    for l in range(CLAT):
        left_ref[4, :, pl.ds(l * LEV, LEV)] = v[8 * l:8 * l + 8, 0:LEV]
        right_ref[4, :, pl.ds(l * LEV, LEV)] = v[8 * l:8 * l + 8, CELL - LEV:]
    halves = jnp.concatenate(split(v), axis=0)
    rows = jnp.concatenate([halves, halves], axis=1)
    for slot in range(SPAN):
        wide = jnp.dot(rows, w_ref[slot], preferred_element_type=F32)
        wide = wide[:64] + wide[64:]
        lat = mask_ref[slot]
        total = jnp.where(lat == 0, wide[0:8], 0.0)
        for l in range(1, CLAT):
            total = total + jnp.where(lat == l, wide[8 * l:8 * l + 8], 0.0)
        own_ref[slot] = total
        if slot >= 1:
            left_ref[slot - 1] = total
        if slot <= 3:
            right_ref[slot] = total
        if slot >= 2:
            left2_ref[slot - 2] = total
        if slot <= 2:
            right2_ref[slot] = total


def init_kernel(z2, z0, z1, z3, z4, lat_ref, w_ref, v_ref, mask_ref):
    sums, lats = [], []
    sub = lax.broadcasted_iota(jnp.int32, (8, SLOT), 0)
    for slot, z_ref in enumerate((z0, z1, z2, z3, z4)):
        z = z_ref[...]
        begin = jnp.broadcast_to(z[S:S + 1, :], (8, SLOT))
        present = (begin <= slot) & (begin + (NT - 1) >= slot)
        lat = jnp.where(present, lat_ref[slot], -1)
        mask_ref[slot] = lat
        lats.append(lat)
        sums.append(jnp.where(sub < S, z, 0.0))
    v_ref[...] = back_all(sums, lats, w_ref)


def ray_sums(own_ref, plus1, minus1, plus2, minus2):
    sums = []
    for slot in range(SPAN):
        total = own_ref[slot]
        if slot <= 3:
            total = total + plus1[slot]
        if slot >= 1:
            total = total + minus1[slot - 1]
        if slot <= 2:
            total = total + plus2[slot]
        if slot >= 2:
            total = total + minus2[slot - 2]
        sums.append(total)
    return sums


def prior_image(v, plus1, minus1, prior_ref):
    west = jnp.concatenate([minus1[4, :, l * LEV:(l + 1) * LEV] for l in range(CLAT)], axis=0)
    east = jnp.concatenate([plus1[4, :, l * LEV:(l + 1) * LEV] for l in range(CLAT)], axis=0)
    cols = [west] + [v[:, c * LEV:(c + 1) * LEV] for c in range(CLON)] + [east]
    lane = lax.broadcasted_iota(jnp.int32, (64, LEV), 1)
    pieces = []
    for c in range(CLON):
        here = cols[c + 1]
        below = jnp.where(lane == 0, 0.0, pltpu.roll(here, 1, 1))
        above = jnp.where(lane == LEV - 1, 0.0, pltpu.roll(here, LEV - 1, 1))
        edge = jnp.zeros((8, LEV), F32)
        south_side = jnp.concatenate([edge, here[:56]], axis=0)
        north_side = jnp.concatenate([here[8:], edge], axis=0)
        near = cols[c] + cols[c + 2] + below + above + south_side + north_side
        pieces.append(prior_ref[...] * (6.0 * here - near))
    return jnp.concatenate(pieces, axis=1)


def step_kernel(v_ref, own_ref, plus1, minus1, plus2, minus2, mask_ref, w_ref, gram_ref, prior_ref, out_ref):
    lats = [mask_ref[slot] for slot in range(SPAN)]
    image = back_all(ray_sums(own_ref, plus1, minus1, plus2, minus2), lats, w_ref)
    image = jnp.dot(gram_ref[...], image, precision=highest, preferred_element_type=F32)
    out_ref[...] = image + prior_image(v_ref[...], plus1, minus1, prior_ref)


PAIRS = [(i, j) for i in range(ITERS) for j in range(i, ITERS)] + [(ITERS - 1, ITERS)]


def last_kernel(side_ref, part_ref, first, second, prior_ref, *refs):
    earlier, (out_ref, pair_ref) = refs[:ITERS], refs[ITERS:]
    v = with_faces(side_ref[0] == 1, part_ref[...], first[...], second[...], prior_ref)
    out_ref[...] = v
    vectors = [ref[...] for ref in earlier] + [v]
    lane = lax.broadcasted_iota(jnp.int32, (1, LEV), 1)
    row = jnp.zeros((1, LEV), F32)
    for n, (i, j) in enumerate(PAIRS):
        product = jnp.sum(vectors[i] * vectors[j], axis=0, keepdims=True)
        row = jnp.where(lane == n, jnp.sum(product, axis=1, keepdims=True), row)
    pair_ref[...] = jnp.broadcast_to(row, pair_ref.shape)


def combine_kernel(scale_ref, *refs):
    sums_ref, vector_refs, (x_ref, r_ref, spread) = refs[0], refs[1:ITERS + 2], refs[ITERS + 2:]
    row = jnp.sum(sums_ref[...], axis=0, keepdims=True)
    table = {}
    for n, (i, j) in enumerate(PAIRS):
        table[i, j] = table[j, i] = row[:, n:n + 1]
    for i in range(ITERS - 1):
        table[i, ITERS] = table[i + 1, ITERS - 1]
    scale = scale_ref[0:1, 0:1]
    zero, one = jnp.zeros((1, 1), F32), jnp.ones((1, 1), F32)
    x = [zero] * (ITERS + 1)
    r = [one] + [zero] * ITERS
    d = list(r)

    def form(a, b, na, nb, off):
        total = None
        for i in range(na):
            inner = None
            for j in range(nb):
                term = b[j] * table[i, j + off]
                inner = term if inner is None else inner + term
            term = a[i] * inner
            total = term if total is None else total + term
        return total

    norm = table[0, 0]
    for k in range(ITERS):
        alpha = norm / form(d, d, k + 1, k + 1, 1)
        for i in range(k + 1):
            x[i] = x[i] + alpha * d[i]
            r[i + 1] = r[i + 1] - alpha * d[i]
        if k < ITERS - 1:
            after = form(r, r, k + 2, k + 2, 0)
            ratio = after / norm
            d = [r[i] + ratio * d[i] for i in range(ITERS + 1)]
            norm = after
    x = [scale * value for value in x]
    for c in range(CLON):
        parts = [ref[:, c * LEV:(c + 1) * LEV] for ref in vector_refs]
        total = x[0] * parts[0]
        for i in range(1, ITERS):
            total = total + x[i] * parts[i]
        spread[0, c] = total
        total = r[0] * parts[0]
        for i in range(1, ITERS + 1):
            total = total + r[i] * parts[i]
        spread[1, c] = total
        for s in range(S):
            x_ref[s, c] = spread[0, c, pl.ds(s, CLAT, stride=8), :]
            r_ref[s, c] = spread[1, c, pl.ds(s, CLAT, stride=8), :]


def shape(*dims, dtype=F32):
    return jax.ShapeDtypeStruct(dims, dtype)


def call(kernel, outs, n_in, scalar=False, scratch=(), work=None):
    return pl.pallas_call(
        kernel,
        out_shape=outs,
        in_specs=([sspec()] if scalar else []) + [vspec()] * n_in,
        out_specs=[vspec()] * len(outs),
        scratch_shapes=scratch,
        compiler_params=LIMIT,
        cost_estimate=work,
    )


MATMUL = pl.CostEstimate(flops=2 * 128 * 2 * CELL * SPAN * SLOT, transcendentals=0, bytes_accessed=2 * 2 * CELL * SPAN * SLOT)
BUILD = pl.CostEstimate(flops=16 * TILE * CELL * SPAN * SLOT, transcendentals=0, bytes_accessed=4 * 2 * CELL * SPAN * SLOT)
MESSAGES = (shape(SPAN, 8, SLOT), shape(5, 8, SLOT), shape(5, 8, SLOT), shape(3, 8, SLOT), shape(3, 8, SLOT))
FACE = shape(8, CELL)
FIELD = shape(64, CELL)
SENT = MESSAGES + (FACE, FACE)


def pairs_from(start, size):
    route = [(i, i + 1) for i in range(start, size - 1, 2)]
    return route + [(j, i) for i, j in route]


def exchange(own, left, right, left2, right2, first, second):
    n_lat = lax.axis_size("lat")
    plus1 = shift(left, "lon", -1)
    minus1 = shift(right, "lon", 1)
    plus2 = shift(left2, "lon", -2)
    minus2 = shift(right2, "lon", 2)
    first = lax.ppermute(first, "lat", pairs_from(0, n_lat))
    plus1, second = lax.optimization_barrier((plus1, second))
    second = lax.ppermute(second, "lat", pairs_from(1, n_lat))
    return own, plus1, minus1, plus2, minus2, first, second


def fetching(kernel, outs, scratch, values):
    return pl.pallas_call(
        kernel,
        out_shape=outs,
        in_specs=[pl.BlockSpec(memory_space=pltpu.HBM)] * len(values),
        out_specs=[vspec()] * len(outs),
        scratch_shapes=list(scratch) + [pltpu.SemaphoreType.DMA((len(values),))],
        compiler_params=LIMIT,
    )(*[pltpu.with_memory_space_constraint(value, pltpu.HBM) for value in values])


def body(observed, ray_start, tile_cells, tile_lengths, channel_kernel, noise_weight, prior_weight):
    side = (lax.axis_index("lat") & 1).astype(jnp.int32).reshape(1)
    table, gram, prior, scale = fetching(
        table_kernel,
        (shape(TABLE + 8, RAYS), shape(64, 64), shape(64, LEV), shape(8, LEV)),
        (
            pltpu.SMEM((S,), F32),
            pltpu.VMEM((TILE, SPAN * RAYS), jnp.int32),
            pltpu.VMEM((TILE, SPAN * RAYS), F32),
            pltpu.VMEM((S, CHAN), F32),
            pltpu.VMEM((1, CHAN), F32),
            pltpu.VMEM((CHAN, RAYS), F32),
            pltpu.VMEM((1, RAYS), jnp.int32),
        ),
        (prior_weight, tile_cells.T, tile_lengths.T, channel_kernel, noise_weight.reshape(1, CHAN), observed.T, ray_start.reshape(1, RAYS)),
    )
    shards = lax.all_gather(table, "orbit")
    (z,) = call(gather_kernel, (shape(8, SLOT),), 1)(shards)
    z1, z3 = shift(z, "lon", -1), shift(z, "lon", 1)
    z0, z4 = shift(z, "lon", -2), shift(z, "lon", 2)
    w, wt, lat = call(build_kernel, (shape(SPAN, 2 * CELL, SLOT, dtype=BF16), shape(SPAN, SLOT, 2 * CELL, dtype=BF16), shape(SPAN, 8, SLOT, dtype=jnp.int32)), 1, work=BUILD)(shards)
    v, mask = call(init_kernel, (FIELD, shape(SPAN, 8, SLOT, dtype=jnp.int32)), 7, work=MATMUL)(z, z0, z1, z3, z4, lat, wt)
    vectors = [v]
    sent = call(project_first_kernel, SENT, 3, True, work=MATMUL)(side, v, mask, w)
    for turn in range(ITERS):
        *sums, first, second = exchange(*sent)
        (part,) = call(step_kernel, (FIELD,), 10, work=MATMUL)(v, *sums, mask, wt, gram, prior)
        if turn < ITERS - 1:
            v, *sent = call(project_kernel, (FIELD,) + SENT, 6, True, work=MATMUL)(side, part, first, second, prior, mask, w)
            vectors.append(v)
    peers = lax.axis_size("lon") * lax.axis_size("lat")
    v, pairs = call(last_kernel, (FIELD, shape(peers, LEV)), 4 + ITERS, True)(side, part, first, second, prior, *vectors)
    vectors.append(v)
    pairs = lax.all_to_all(pairs, ("lon", "lat"), 0, 0, tiled=True)
    field = shape(S, CLON, CLAT, LEV)
    return tuple(call(combine_kernel, (field, field), ITERS + 3, False, [pltpu.VMEM((2, CLON, 64, LEV), F32)])(scale, pairs, *vectors))


def solution(mesh):
    return jax.shard_map(
        body,
        mesh=mesh,
        in_specs=(
            P(("orbit", "lon", "lat"), None),
            P(("orbit", "lon", "lat")),
            P(("orbit", "lon", "lat"), None),
            P(("orbit", "lon", "lat"), None),
            P(),
            P(),
            P(),
        ),
        out_specs=(P(None, "lon", "lat", None), P(None, "lon", "lat", None)),
        check_vma=False,
    )
```
